32 devices in a mesh: fsdp: 8 (over y, x, core), tp: 4 (over z).
Axes of the slice: x: 2, y: 2, z: 4, core: 2. Of those that a mesh axis runs over, the one named last changes fastest.
Arguments:
- tokens_in: bfloat16 [2, 2560, 2048], P(None, ('fsdp', 'tp')), may hold values from -6 to 6
- out_grad: bfloat16 [2, 2560, 2048], P(None, ('fsdp', 'tp')), may hold values from -6 to 6
- segment_ids: int32 [2, 2560], P(None, 'fsdp'), may hold values from 0 to 2, as said below
- expert_ids: int32 [2, 2560, 2], P(None, 'fsdp'), may hold values from 0 to 3, all different within a row; in each aligned block of 320 rows (0 to 319, 320 to 639, ..., all dimensions but the last counted through in order) at most 200 rows name the same one
- attn_gain: bfloat16 [2048], P(('fsdp', 'tp')), may hold values from 0.5 to 1.5
- w_query: bfloat16 [2048, 2048], P('fsdp', 'tp'), may hold values from -0.1875 to 0.1875
- w_key: bfloat16 [2048, 2048], P('fsdp', 'tp'), may hold values from -0.1875 to 0.1875
- w_value: bfloat16 [2048, 2048], P('fsdp', 'tp'), may hold values from -0.125 to 0.125
- w_output: bfloat16 [2048, 2048], P('tp', 'fsdp'), may hold values from -0.5 to 0.5
- ffn_gain: bfloat16 [2048], P(('fsdp', 'tp')), may hold values from 0.5 to 1.5
- w_router: bfloat16 [2048, 4], P(('fsdp', 'tp')), may hold values from -0.125 to 0.125
- w_gate: bfloat16 [4, 2048, 5632], P(None, 'fsdp', 'tp'), may hold values from -0.125 to 0.125
- w_up: bfloat16 [4, 2048, 5632], P(None, 'fsdp', 'tp'), may hold values from -0.125 to 0.125
- w_down: bfloat16 [4, 5632, 2048], P(None, 'tp', 'fsdp'), may hold values from -0.15625 to 0.15625
Outputs:
- output: bfloat16 [2, 2560, 2048], P(None, ('fsdp', 'tp'))
- input_grad: bfloat16 [2, 2560, 2048], P(None, ('fsdp', 'tp'))
- attn_gain_grad: float32 [2048], P(('fsdp', 'tp'))
- w_query_grad: float32 [2048, 2048], P('fsdp', 'tp')
- w_key_grad: float32 [2048, 2048], P('fsdp', 'tp')
- w_value_grad: float32 [2048, 2048], P('fsdp', 'tp')
- w_output_grad: float32 [2048, 2048], P('tp', 'fsdp')
- ffn_gain_grad: float32 [2048], P(('fsdp', 'tp'))
- w_router_grad: float32 [2048, 4], P(('fsdp', 'tp'))
- w_gate_grad: float32 [4, 2048, 5632], P(None, 'fsdp', 'tp')
- w_up_grad: float32 [4, 2048, 5632], P(None, 'fsdp', 'tp')
- w_down_grad: float32 [4, 5632, 2048], P(None, 'tp', 'fsdp')
The draws below stay inside these ranges and needn't reach their ends.
Inputs may be any that keep to these rules, and one draw needn't show every extreme that they name: `expert_ids`: each row names two different experts. In each aligned block of 320 rows (one group of a micro-batch) no expert is named by more than 200 rows, a bound that some block reaches. `segment_ids`: in each aligned block of 320 rows (one group of a micro-batch) the first 192 rows have segment 0; the other rows hold segments 1 to 2 in order, never falling, each with one row or more.
All inputs are finite; a program needn't handle non-finite values.
Results may differ from the reference program's by a relative error of at most 0.025.
Values may be sent and summed in bfloat16 or wider, within the bound.
No kernel may reach another device: no remote copies, remote signals or barrier semaphores. Data moves between devices by JAX's collectives and lax.ppermute only.
A program may use at most 384 MiB of HBM per device.

```python
import math
import jax
import jax.numpy as jnp
import numpy as np
from jax import lax

D = 2048
H = 16
HD = 128
FF = 5632
E = 4
PROMPT = 192
CONT_TOK = 128
CONTS = 2
MB = 2
GROUP = 320
CAP = 200
TOKENS = 2560


def draw_segment_ids(key, part):
    group_count = MB * (TOKENS // GROUP)
    group_keys = jax.random.split(key, group_count)

    def one_group(group_key):
        cut_points = jax.random.permutation(group_key, CONT_TOK - 1)[:CONTS - 1] + 1
        offsets = jnp.arange(CONT_TOK, dtype=jnp.int32)
        segment_of = 1 + jnp.sum((offsets[:, None] >= cut_points[None, :]).astype(jnp.int32), axis=1)
        return jnp.concatenate([jnp.zeros((PROMPT,), jnp.int32), segment_of.astype(jnp.int32)])
    return jax.vmap(one_group)(group_keys).reshape(MB, TOKENS).astype(jnp.int32)


def strengthened(values, key, source, target, parts, factor):
    def block_of(dim):
        return (jnp.arange(values.shape[dim]) // (values.shape[dim] // parts)).reshape((-1,) + (1,) * (values.ndim - 1 - dim))

    one_side = jax.random.permutation(key, parts)[block_of(target)]
    other_side = (block_of(target) + parts // 2) % parts
    return jnp.where((block_of(source) == one_side) | (block_of(source) == other_side), factor * values, values)


def shard_levels(stream_key, dims, pieces, smallest, largest):
    factor_of, own = 1.0, jax.random.fold_in(stream_key, 6)
    for dim, shards_of in pieces:
        steps = jnp.exp(jax.random.uniform(jax.random.fold_in(own, dim), (shards_of,), jnp.float32, smallest / len(pieces), largest / len(pieces)))
        factor_of = factor_of * jnp.repeat(steps, dims[dim] // shards_of).reshape([-1 if axis == dim else 1 for axis in range(len(dims))])
    return factor_of


def assign_block(key, own, number, rows, count, top, limit, lean):
    sequence = jax.random.permutation(key, count)
    crowded, ordinary = portions_of(count, rows * top, limit, lean, True), portions_of(count, rows * top, limit, lean, False)
    places = jnp.arange(count)

    def named(sizes, rotation):
        used = int((sizes > 0).sum())
        fixed = max(1, used // 4)
        shifted = fixed + (places - fixed + rotation * (used - fixed)) % max(1, count - fixed)
        return jnp.zeros((count,), jnp.int32).at[sequence[jnp.where(places < fixed, places, shifted)]].set(jnp.asarray(sizes, jnp.int32))

    sizes = jnp.where(number % 4 == 0, named(crowded, number // 4), named(ordinary, number - number // 4 - 1))
    mixed = jax.random.permutation(jax.random.fold_in(own, 3), count)
    giver, taker = mixed[0:count // 2 * 2:2], mixed[1:count // 2 * 2:2]
    margin = jnp.minimum(sizes[giver] - 1, limit - sizes[taker]) // 2
    margin = jnp.where((giver == sequence[0]) | (taker == sequence[0]) | (sizes[taker] == 0), 0, jnp.maximum(margin, 0))
    shifted = jax.random.randint(jax.random.fold_in(own, 4), (count // 2,), 0, 1 << 20) % (margin + 1)
    sizes = sizes.at[giver].add(-shifted).at[taker].add(shifted)
    labels = jnp.searchsorted(jnp.cumsum(sizes), jnp.arange(rows * top), side="right").astype(jnp.int32)
    listing = labels.reshape(top, rows).T
    listing = listing[jax.random.permutation(jax.random.fold_in(own, 1), rows)]
    rotation = jax.random.randint(jax.random.fold_in(own, 2), (rows, 1), 0, top)
    return jnp.take_along_axis(listing, (jnp.arange(top)[None, :] + rotation) % top, axis=1)


def portions_of(number_of, total, bound, skew, full):
    portions = [(1 << 20) // math.isqrt(grade ** skew) + 1 for grade in range(1, number_of + 1)]
    largest = bound if full else min(bound, max(-(-total // number_of), total * portions[0] // sum(portions)))
    least = 1 if total - largest >= number_of - 1 else 0
    holding, spare = [largest] + [least] * (number_of - 1), total - largest - least * (number_of - 1)
    while spare > 0:
        free = [i for i in range(1, number_of) if holding[i] < largest] or [i for i in range(1, number_of) if holding[i] < bound]
        mass, remaining = sum([portions[i] for i in free]), spare
        for i in free:
            extra = min(bound - holding[i], max(1, remaining * portions[i] // mass), spare)
            holding[i] = holding[i] + extra
            spare = spare - extra
    return np.array(holding)


def centred(stream_key, shape, spread, limit, cuts=(), held_as=jnp.bfloat16):
    entries = spread * jax.random.normal(stream_key, shape, jnp.float32)
    if cuts:
        entries = entries * shard_levels(stream_key, shape, cuts, -0.22, 0.18)
    return jnp.clip(entries, -limit, limit).astype(held_as)


def gaussian_with(stream_key, shape, spread, bound, cuts, heavy, kind=jnp.bfloat16):
    entries = spread * jax.random.normal(stream_key, shape, jnp.float32)
    if cuts:
        entries = entries * shard_levels(stream_key, shape, cuts, -0.22, 0.18)
    return jnp.clip(strengthened(entries, jax.random.fold_in(stream_key, 3), *heavy), -bound, bound).astype(kind)


def setup_inputs(seed: int = 0) -> dict:
    key_list = jax.random.split(jax.random.key(seed), 15)
    tokens_in = centred(key_list[0], (MB, TOKENS, D), 1.0, 6.0, ((1, 32),))
    out_grad = gaussian_with(key_list[1], (MB, TOKENS, D), 1.0, 6.0, ((1, 32),), (1, 2, 32, 2.75))
    segment_ids = draw_segment_ids(jax.random.fold_in(key_list[14], 71), 0)
    expert_ids_keys = jax.random.split(jax.random.fold_in(key_list[3], 1), MB * TOKENS // GROUP)
    expert_ids_turns = jax.random.permutation(jax.random.fold_in(key_list[3], 3), MB * TOKENS // GROUP)
    expert_ids = jax.vmap(lambda own, number: assign_block(jax.random.fold_in(key_list[3], 2), own, number, GROUP, E, 2, CAP, 1))(expert_ids_keys, expert_ids_turns).reshape((MB, TOKENS, 2))
    attn_gain = jnp.clip(1.0 + 0.1 * jax.random.normal(key_list[4], (D,), jnp.float32), 0.5, 1.5).astype(jnp.bfloat16)
    w_query = centred(key_list[5], (D, H * HD), (D // 2) ** -0.5, 0.1875, ((0, 8), (1, 4)))
    w_key = centred(key_list[6], (D, H * HD), (D // 2) ** -0.5, 0.1875, ((0, 8), (1, 4)))
    w_value = centred(key_list[7], (D, H * HD), D ** -0.5, 0.125, ((0, 8), (1, 4)))
    w_output = centred(key_list[8], (H * HD, D), (H * HD // 16) ** -0.5, 0.5, ((0, 4), (1, 8)))
    ffn_gain = jnp.clip(1.0 + 0.1 * jax.random.normal(key_list[9], (D,), jnp.float32), 0.5, 1.5).astype(jnp.bfloat16)
    w_router = centred(key_list[10], (D, E), D ** -0.5, 0.125, ((0, 32),))
    w_gate = centred(key_list[11], (E, D, FF), D ** -0.5, 0.125, ((1, 8), (2, 4)))
    w_up = centred(key_list[12], (E, D, FF), D ** -0.5, 0.125, ((1, 8), (2, 4)))
    w_down = centred(key_list[13], (E, FF, D), (FF // 4) ** -0.5, 0.15625, ((1, 4), (2, 8)))
    return dict(tokens_in=tokens_in, out_grad=out_grad, segment_ids=segment_ids, expert_ids=expert_ids, attn_gain=attn_gain, w_query=w_query, w_key=w_key, w_value=w_value, w_output=w_output, ffn_gain=ffn_gain, w_router=w_router, w_gate=w_gate, w_up=w_up, w_down=w_down)


EPSILON = 1e-05
MASKED = -1e+30
HIGHEST = lax.Precision.HIGHEST

@jax.custom_vjp
def low(v):
    return lax.optimization_barrier(v.astype(jnp.bfloat16)).astype(jnp.float32)

@jax.custom_vjp
def low_back(v):
    return v

def low_keep(v):
    return (low(v), None)

def low_pass(kept, grad):
    return (grad,)

def back_keep(v):
    return (v, None)

def back_low(kept, grad):
    return (low(grad),)
low.defvjp(low_keep, low_pass)
low_back.defvjp(back_keep, back_low)

def inverse_rms(values):
    return lax.rsqrt(lax.optimization_barrier(jnp.mean(values * values, axis=-1, keepdims=True)) + EPSILON)

def rotary_tables(segments, head_dim):
    row_index = jnp.arange(segments.shape[0], dtype=jnp.int32)
    earlier = lax.optimization_barrier(jnp.sum((segments[None, :] < segments[:, None]).astype(jnp.int32), axis=1))
    prompt_rows = jnp.sum((segments == 0).astype(jnp.int32))
    position = row_index - earlier + jnp.where(segments > 0, prompt_rows, 0)
    frequency = 10000.0 ** (-(jnp.arange(head_dim // 2, dtype=jnp.float32) * 2.0) / head_dim)
    angles = position.astype(jnp.float32)[:, None] * frequency[None, :]
    return (jnp.cos(angles)[:, None, :], jnp.sin(angles)[:, None, :])

def rotate(values, cosine_table, sine_table):
    half_dim = values.shape[-1] // 2
    first_half = values[..., :half_dim]
    second_half = values[..., half_dim:]
    return jnp.concatenate([first_half * cosine_table - second_half * sine_table, second_half * cosine_table + first_half * sine_table], axis=-1)

def attend_mask(segments):
    row_index = jnp.arange(segments.shape[0], dtype=jnp.int32)
    causal = row_index[None, :] <= row_index[:, None]
    same_doc = (segments[None, :] == 0) | (segments[None, :] == segments[:, None])
    return causal & same_doc

def attend_packed(packed):
    query, keys, values, segments = packed
    cosine_table, sine_table = rotary_tables(segments, HD)
    query_rot = low(rotate(query, cosine_table, sine_table) * (1.0 / math.sqrt(HD)))
    keys_rot = low(rotate(keys, cosine_table, sine_table))
    values_low = low(values)
    scores = low_back(jnp.einsum('qhd,khd->hqk', query_rot, keys_rot, precision=HIGHEST))
    scores = jnp.where(attend_mask(segments)[None], scores, MASKED)
    row_max = lax.optimization_barrier(jnp.max(scores, axis=-1, keepdims=True))
    exps = jnp.exp(scores - row_max)
    probs = exps / lax.optimization_barrier(jnp.sum(exps, axis=-1, keepdims=True))
    context = jnp.einsum('hqk,khd->qhd', low(probs), values_low, precision=HIGHEST)
    return low(low_back(context))

def block(inputs, segments, routes, gain_one, query_w, key_w, value_w, output_w, gain_two, router, gate_w, up_w, down_w):
    rows = inputs.shape[0]
    groups = rows // GROUP
    hidden_one = low(inputs * inverse_rms(inputs) * gain_one)
    query = low_back(jnp.dot(hidden_one, query_w, precision=HIGHEST))
    keys = low_back(jnp.dot(hidden_one, key_w, precision=HIGHEST))
    values = low_back(jnp.dot(hidden_one, value_w, precision=HIGHEST))
    shape_four = (groups, GROUP, H, HD)
    context = lax.map(jax.checkpoint(attend_packed), (query.reshape(shape_four), keys.reshape(shape_four), values.reshape(shape_four), segments.reshape(groups, GROUP)))
    attn = low_back(jnp.dot(context.reshape(rows, H * HD), output_w, precision=HIGHEST))
    middle = inputs + attn
    hidden_two = low(middle * inverse_rms(middle) * gain_two)
    logits = jnp.dot(hidden_two, router, precision=HIGHEST)
    one_hot = (routes[:, :, None] == jnp.arange(E, dtype=jnp.int32)[None, None, :]).astype(jnp.float32)
    chosen = lax.optimization_barrier(jnp.sum(one_hot * logits[:, None, :], axis=-1))
    chosen_max = lax.optimization_barrier(jnp.max(chosen, axis=-1, keepdims=True))
    chosen_exp = jnp.exp(chosen - chosen_max)
    gate_weights = chosen_exp / lax.optimization_barrier(jnp.sum(chosen_exp, axis=-1, keepdims=True))
    expert_weight = lax.optimization_barrier(jnp.sum(gate_weights[:, :, None] * one_hot, axis=1))
    mixed = jnp.zeros_like(middle)
    for expert in range(E):
        gate_pre = low_back(jnp.dot(hidden_two, gate_w[expert], precision=HIGHEST))
        up_pre = low_back(jnp.dot(hidden_two, up_w[expert], precision=HIGHEST))
        activated = low(jax.nn.silu(gate_pre) * up_pre)
        expert_out = low_back(jnp.dot(activated, down_w[expert], precision=HIGHEST))
        mixed = mixed + expert_weight[:, expert:expert + 1] * expert_out
    return middle + mixed

def reference(tokens_in, out_grad, segment_ids, expert_ids, attn_gain, w_query, w_key, w_value, w_output, ffn_gain, w_router, w_gate, w_up, w_down):
    params = tuple((item.astype(jnp.float32) for item in (attn_gain, w_query, w_key, w_value, w_output, ffn_gain, w_router, w_gate, w_up, w_down)))
    outputs = []
    input_grads = []
    totals = None
    for batch_index in range(MB):
        segments = segment_ids[batch_index]
        routes = expert_ids[batch_index]

        def closed(inputs, *weights):
            return block(inputs, segments, routes, *weights)
        result, pullback = jax.vjp(closed, tokens_in[batch_index].astype(jnp.float32), *params)
        grads = pullback(out_grad[batch_index].astype(jnp.float32))
        outputs.append(result.astype(jnp.bfloat16))
        input_grads.append(grads[0].astype(jnp.bfloat16))
        if totals is None:
            totals = tuple(grads[1:])
        else:
            totals = tuple(jax.tree.map(jnp.add, totals, tuple(grads[1:])))
    return (jnp.stack(outputs), jnp.stack(input_grads), totals[0], totals[1], totals[2], totals[3], totals[4], totals[5], totals[6], totals[7], totals[8], totals[9])
```

```python
import math

import jax
import jax.numpy as jnp
from jax import lax
from jax.sharding import PartitionSpec as P

HD = 128
CAP = 200
EPSILON = 1e-05
MASKED = -1e30
HIGHEST = lax.Precision.HIGHEST
BF16 = jnp.bfloat16
F32 = jnp.float32


def inverse_rms(values):
    return lax.rsqrt(jnp.mean(values * values, axis=-1, keepdims=True) + EPSILON)


def norm_backward(inputs, gain, grad_out):
    inv_scale = inverse_rms(inputs)
    gain_grad = jnp.sum(grad_out * inputs * inv_scale, axis=(0, 1))
    scaled = grad_out * gain
    input_grad = inv_scale * scaled - inputs * (inv_scale * inv_scale * inv_scale) * jnp.mean(
        scaled * inputs, axis=-1, keepdims=True
    )
    return (input_grad, gain_grad)


def rotary_tables(segments, head_dim):
    row_index = jnp.arange(segments.shape[1], dtype=jnp.int32)[None, :]
    earlier = jnp.sum((segments[:, None, :] < segments[:, :, None]).astype(jnp.int32), axis=2)
    prompt_rows = jnp.sum((segments == 0).astype(jnp.int32), axis=1, keepdims=True)
    position = row_index - earlier + jnp.where(segments > 0, prompt_rows, 0)
    frequency = 10000.0 ** (-(jnp.arange(head_dim // 2, dtype=F32) * 2.0) / head_dim)
    angles = position.astype(F32)[:, :, None] * frequency[None, None, :]
    return (jnp.cos(angles)[:, :, None, :], jnp.sin(angles)[:, :, None, :])


def rotate(values, cosine_table, sine_table):
    half_dim = values.shape[-1] // 2
    first_half = values[..., :half_dim]
    second_half = values[..., half_dim:]
    return jnp.concatenate(
        [
            first_half * cosine_table - second_half * sine_table,
            second_half * cosine_table + first_half * sine_table,
        ],
        axis=-1,
    )


def attend_mask(segments):
    row_index = jnp.arange(segments.shape[1], dtype=jnp.int32)
    causal = (row_index[None, :] <= row_index[:, None])[None]
    same_doc = (segments[:, None, :] == 0) | (segments[:, None, :] == segments[:, :, None])
    return causal & same_doc


def tp_gather(own):
    count = lax.axis_size("tp")
    rank = lax.axis_index("tp")
    micro, rows, width = own.shape
    full = jnp.zeros((micro, count * rows, width), own.dtype)
    pieces = [own] + [
        lax.ppermute(own, "tp", [(i, (i + k) % count) for i in range(count)])
        for k in range(1, count)
    ]
    for k, piece in enumerate(pieces):
        place = lax.rem(rank - k + count, count) * rows
        full = lax.dynamic_update_slice_in_dim(full, piece, place, 1)
    return full


def tp_scatter(part):
    count = lax.axis_size("tp")
    rank = lax.axis_index("tp")
    rows = part.shape[1] // count
    total = lax.dynamic_slice_in_dim(part, rank * rows, rows, 1).astype(F32)
    for k in range(1, count):
        place = lax.rem(rank + k, count) * rows
        piece = lax.dynamic_slice_in_dim(part, place, rows, 1)
        got = lax.ppermute(piece, "tp", [(i, (i + k) % count) for i in range(count)])
        total = total + got.astype(F32)
    return total


def dot(spec, a, b):
    return jnp.einsum(spec, a, b, preferred_element_type=F32)


def per_device(
    tokens_in,
    out_grad,
    segment_ids,
    expert_ids,
    attn_gain,
    w_query,
    w_key,
    w_value,
    w_output,
    ffn_gain,
    w_router,
    w_gate,
    w_up,
    w_down,
):
    tensor_count = lax.axis_size("tp")
    tensor_rank = lax.axis_index("tp")
    micro, own_rows, width = tokens_in.shape
    group_rows = own_rows * tensor_count
    experts = w_gate.shape[0]
    units = w_gate.shape[2]
    head_width = w_query.shape[1]
    heads = head_width // HD
    query_scale = 1.0 / math.sqrt(HD)
    rows = micro * group_rows
    slots = micro * CAP

    attn_set = lax.all_gather(
        jnp.concatenate([w_query, w_key, w_value, w_output.T], axis=1), "fsdp", axis=0, tiled=True
    )
    small = lax.all_gather(
        jnp.concatenate([attn_gain[:, None], ffn_gain[:, None], w_router], axis=1),
        ("fsdp", "tp"),
        axis=0,
        tiled=True,
    )
    expert_sets = [
        lax.all_gather(
            jnp.concatenate([w_gate[e], w_up[e], w_down[e].T], axis=1), "fsdp", axis=0, tiled=True
        )
        for e in range(experts)
    ]
    gain_one = small[:, 0].astype(F32)
    gain_two = small[:, 1].astype(F32)
    router = small[:, 2:]

    tokens_full = tp_gather(tokens_in).astype(F32)
    hidden_one = (tokens_full * inverse_rms(tokens_full) * gain_one).astype(BF16)
    hidden_one = hidden_one.reshape(rows, width)
    cosine_table, sine_table = rotary_tables(segment_ids, HD)
    allowed = attend_mask(segment_ids)
    qkv = dot("td,de->te", hidden_one, attn_set[:, : 3 * head_width])
    four = (micro, group_rows, heads, HD)
    query_raw = qkv[:, :head_width].reshape(four)
    key_raw = qkv[:, head_width : 2 * head_width].reshape(four)
    values_low = qkv[:, 2 * head_width :].reshape(four).astype(BF16)
    query_rot = (rotate(query_raw, cosine_table, sine_table) * query_scale).astype(BF16)
    keys_rot = rotate(key_raw, cosine_table, sine_table).astype(BF16)
    scores = dot("mqhd,mkhd->mhqk", query_rot, keys_rot)
    scores = jnp.where(allowed[:, None], scores, MASKED)
    exps = jnp.exp(scores - jnp.max(scores, axis=-1, keepdims=True))
    probs = exps / jnp.sum(exps, axis=-1, keepdims=True)
    probs_low = probs.astype(BF16)
    context = dot("mhqk,mkhd->mqhd", probs_low, values_low).reshape(rows, head_width).astype(BF16)
    attn_part = dot("te,de->td", context, attn_set[:, 3 * head_width :]).astype(BF16)
    inputs = tokens_in.astype(F32)
    middle = inputs + tp_scatter(attn_part.reshape(micro, group_rows, width))
    normed_two = (middle * inverse_rms(middle) * gain_two).astype(BF16)
    hidden_two = tp_gather(normed_two)
    grad_full = tp_gather(out_grad)

    logits = dot("mtd,de->mte", hidden_two, router)
    named = jnp.any(
        expert_ids[:, :, :, None] == jnp.arange(experts, dtype=jnp.int32), axis=2
    )
    chosen = jnp.where(named, logits, MASKED)
    chosen_exp = jnp.where(named, jnp.exp(chosen - jnp.max(chosen, axis=-1, keepdims=True)), 0.0)
    gates = chosen_exp / jnp.sum(chosen_exp, axis=-1, keepdims=True)
    row_index = jnp.arange(group_rows, dtype=jnp.int32)
    before = (row_index[None, :] < row_index[:, None]).astype(BF16)
    slot_of = dot("ts,mse->met", before, named.astype(BF16)).astype(jnp.int32)
    slot_of = jnp.where(jnp.swapaxes(named, 1, 2), slot_of, -1)
    picks = slot_of[:, :, None, :] == jnp.arange(CAP, dtype=jnp.int32)[None, None, :, None]
    slot_gates = jnp.sum(
        jnp.where(picks, jnp.swapaxes(gates, 1, 2)[:, :, None, :], 0.0), axis=-1, keepdims=True
    )
    picks_low = picks.astype(BF16)

    weighted_outs = []
    gate_grad_slots = []
    routed_grads = []
    expert_grads = []
    for e in range(experts):
        weights = expert_sets[e]
        gate_up = weights[:, : 2 * units]
        down = weights[:, 2 * units :]
        pick = picks_low[:, e]
        if e:
            pick, packed = lax.optimization_barrier((pick, packed))
            expert_grads.append(lax.psum_scatter(packed, "fsdp", scatter_dimension=0, tiled=True))
        routed = dot("mst,mtd->msd", pick, hidden_two).astype(BF16).reshape(slots, width)
        grad_slot = dot("mst,mtd->msd", pick, grad_full)
        slot_gate = slot_gates[:, e]
        slot_grad = (slot_gate * grad_slot).astype(BF16).reshape(slots, width)
        pre = dot("sd,df->sf", routed, gate_up)
        gate_pre = pre[:, :units]
        up_pre = pre[:, units:]
        gate_sigmoid = jax.nn.sigmoid(gate_pre)
        silu = gate_pre * gate_sigmoid
        activated = (silu * up_pre).astype(BF16)
        expert_out = dot("sf,df->sd", activated, down).reshape(micro, CAP, width)
        weighted_outs.append((slot_gate * expert_out).astype(BF16))
        gate_grad_slots.append(jnp.sum(expert_out * grad_slot, axis=-1))
        act_grad = dot("sd,df->sf", slot_grad, down)
        pre_grad = jnp.concatenate(
            [
                (act_grad * up_pre * gate_sigmoid * (1.0 + gate_pre * (1.0 - gate_sigmoid))).astype(
                    BF16
                ),
                (act_grad * silu).astype(BF16),
            ],
            axis=1,
        )
        packed = jnp.concatenate(
            [
                dot("sd,sf->df", routed, pre_grad).astype(BF16),
                dot("sd,sf->df", slot_grad, activated).astype(BF16),
            ],
            axis=1,
        )
        routed_grads.append(
            dot("sf,df->sd", pre_grad, gate_up).astype(BF16).reshape(micro, CAP, width)
        )
    picks_low, packed = lax.optimization_barrier((picks_low, packed))
    expert_grads.append(lax.psum_scatter(packed, "fsdp", scatter_dimension=0, tiled=True))
    flat_picks = picks_low.reshape(micro, experts * CAP, group_rows)
    token_grad = dot("mst,msd->mtd", flat_picks, jnp.concatenate(routed_grads, axis=1))
    gate_grad_part = jnp.sum(
        jnp.where(picks, jnp.stack(gate_grad_slots, axis=1)[:, :, :, None], 0.0), axis=2
    )
    gate_grad_part = jnp.pad(jnp.swapaxes(gate_grad_part, 1, 2), ((0, 0), (0, 0), (0, HD - experts)))
    summed = tp_scatter(jnp.concatenate([token_grad, gate_grad_part], axis=-1).astype(BF16))
    moe_part = dot("mst,msd->mtd", flat_picks, jnp.concatenate(weighted_outs, axis=1))
    output = (middle + tp_scatter(moe_part.astype(BF16))).astype(BF16)

    gates_own = lax.dynamic_slice_in_dim(gates, tensor_rank * own_rows, own_rows, 1)
    gate_grad = summed[:, :, width : width + experts]
    logit_grad = gates_own * (
        gate_grad - jnp.sum(gates_own * gate_grad, axis=-1, keepdims=True)
    )
    router_grad = jnp.einsum(
        "mtd,mte->de", normed_two.astype(F32), logit_grad, precision=HIGHEST
    )
    hidden_two_grad = summed[:, :, :width] + jnp.einsum(
        "mte,de->mtd", logit_grad, router.astype(F32), precision=HIGHEST
    )
    middle_norm_grad, gain_two_grad = norm_backward(middle, gain_two, hidden_two_grad)
    middle_grad = middle_norm_grad + out_grad.astype(F32)

    attn_grad = tp_gather(middle_grad.astype(BF16)).reshape(rows, width)
    context_grad = dot("td,de->te", attn_grad, attn_set[:, 3 * head_width :])
    context_grad = context_grad.astype(BF16).reshape(four)
    prob_grad = dot("mqhd,mkhd->mhqk", context_grad, values_low)
    row_delta = jnp.sum(probs * prob_grad, axis=-1, keepdims=True)
    score_grad = (probs * (prob_grad - row_delta)).astype(BF16)
    query_grad = rotate(
        dot("mhqk,mkhd->mqhd", score_grad, keys_rot) * query_scale, cosine_table, -sine_table
    )
    key_grad = rotate(dot("mhqk,mqhd->mkhd", score_grad, query_rot), cosine_table, -sine_table)
    value_grad = dot("mhqk,mqhd->mkhd", probs_low, context_grad)
    qkv_grad = jnp.concatenate(
        [item.astype(BF16).reshape(rows, head_width) for item in (query_grad, key_grad, value_grad)],
        axis=1,
    )
    hidden_part = dot("te,de->td", qkv_grad, attn_set[:, : 3 * head_width]).astype(BF16)
    hidden_one_grad = tp_scatter(hidden_part.reshape(micro, group_rows, width))
    inner_grad, gain_one_grad = norm_backward(inputs, gain_one, hidden_one_grad)
    input_grad = (middle_grad + inner_grad).astype(BF16)
    small_part = jnp.concatenate(
        [gain_one_grad[:, None], gain_two_grad[:, None], router_grad], axis=1
    )
    small_width = small_part.shape[1]
    attn_packed = jnp.concatenate(
        [
            dot("td,te->de", hidden_one, qkv_grad).astype(BF16),
            dot("td,te->de", attn_grad, context).astype(BF16),
            jnp.pad(small_part, ((0, 0), (0, HD - small_width))).astype(BF16),
        ],
        axis=1,
    )
    attn_packed, expert_grads = lax.optimization_barrier((attn_packed, expert_grads))
    attn_grads = lax.psum_scatter(attn_packed, "fsdp", scatter_dimension=0, tiled=True)
    small_grads = tp_scatter(attn_grads[None, :, 4 * head_width :])[0]
    attn_grads = attn_grads.astype(F32)
    return (
        output,
        input_grad,
        small_grads[:, 0],
        attn_grads[:, :head_width],
        attn_grads[:, head_width : 2 * head_width],
        attn_grads[:, 2 * head_width : 3 * head_width],
        attn_grads[:, 3 * head_width : 4 * head_width].T,
        small_grads[:, 1],
        small_grads[:, 2:small_width],
        jnp.stack([item[:, :units] for item in expert_grads]).astype(F32),
        jnp.stack([item[:, units : 2 * units] for item in expert_grads]).astype(F32),
        jnp.stack([item[:, 2 * units :].T for item in expert_grads]).astype(F32),
    )


def solution(mesh):
    return jax.shard_map(
        per_device,
        mesh=mesh,
        in_specs=(
            P(None, ("fsdp", "tp"), None),
            P(None, ("fsdp", "tp"), None),
            P(None, "fsdp"),
            P(None, "fsdp", None),
            P(("fsdp", "tp")),
            P("fsdp", "tp"),
            P("fsdp", "tp"),
            P("fsdp", "tp"),
            P("tp", "fsdp"),
            P(("fsdp", "tp")),
            P(("fsdp", "tp"), None),
            P(None, "fsdp", "tp"),
            P(None, "fsdp", "tp"),
            P(None, "tp", "fsdp"),
        ),
        out_specs=(
            P(None, ("fsdp", "tp"), None),
            P(None, ("fsdp", "tp"), None),
            P(("fsdp", "tp")),
            P("fsdp", "tp"),
            P("fsdp", "tp"),
            P("fsdp", "tp"),
            P("tp", "fsdp"),
            P(("fsdp", "tp")),
            P(("fsdp", "tp"), None),
            P(None, "fsdp", "tp"),
            P(None, "fsdp", "tp"),
            P(None, "tp", "fsdp"),
        ),
        check_vma=False,
    )
```

```python
import math

import jax
import jax.numpy as jnp
from jax import lax
from jax.sharding import PartitionSpec as P


HD = 128
CAP = 200
PAIR = 2
EPSILON = 1e-05
MASKED = -1e30
HIGHEST = lax.Precision.HIGHEST
BF16 = jnp.bfloat16
F32 = jnp.float32


def inverse_rms(values):
    return lax.rsqrt(jnp.mean(values * values, axis=-1, keepdims=True) + EPSILON)


def norm_backward(inputs, gain, grad_out):
    inv_scale = inverse_rms(inputs)
    gain_grad = jnp.sum(grad_out * inputs * inv_scale, axis=(0, 1))
    scaled = grad_out * gain
    input_grad = inv_scale * scaled - inputs * (inv_scale * inv_scale * inv_scale) * jnp.mean(
        scaled * inputs, axis=-1, keepdims=True
    )
    return (input_grad, gain_grad)


def rotary_tables(segments, head_dim):
    row_index = jnp.arange(segments.shape[1], dtype=jnp.int32)[None, :]
    earlier = jnp.sum((segments[:, None, :] < segments[:, :, None]).astype(jnp.int32), axis=2)
    prompt_rows = jnp.sum((segments == 0).astype(jnp.int32), axis=1, keepdims=True)
    position = row_index - earlier + jnp.where(segments > 0, prompt_rows, 0)
    frequency = 10000.0 ** (-(jnp.arange(head_dim // 2, dtype=F32) * 2.0) / head_dim)
    angles = position.astype(F32)[:, :, None] * frequency[None, None, :]
    return (jnp.cos(angles)[:, :, None, :], jnp.sin(angles)[:, :, None, :])


def rotate(values, cosine_table, sine_table):
    half_dim = values.shape[-1] // 2
    first_half = values[..., :half_dim]
    second_half = values[..., half_dim:]
    return jnp.concatenate(
        [
            first_half * cosine_table - second_half * sine_table,
            second_half * cosine_table + first_half * sine_table,
        ],
        axis=-1,
    )


def attend_mask(segments):
    row_index = jnp.arange(segments.shape[1], dtype=jnp.int32)
    causal = (row_index[None, :] <= row_index[:, None])[None]
    same_doc = (segments[:, None, :] == 0) | (segments[:, None, :] == segments[:, :, None])
    return causal & same_doc


def tp_gather(own):
    count = lax.axis_size("tp")
    rank = lax.axis_index("tp")
    micro, rows, width = own.shape
    full = jnp.zeros((micro, count * rows, width), own.dtype)
    pieces = [own] + [
        lax.ppermute(own, "tp", [(i, (i + k) % count) for i in range(count)])
        for k in range(1, count)
    ]
    for k, piece in enumerate(pieces):
        place = lax.rem(rank - k + count, count) * rows
        full = lax.dynamic_update_slice_in_dim(full, piece, place, 1)
    return full


def tp_scatter(part):
    count = lax.axis_size("tp")
    rank = lax.axis_index("tp")
    rows = part.shape[1] // count
    total = lax.dynamic_slice_in_dim(part, rank * rows, rows, 1).astype(F32)
    for k in range(1, count):
        place = lax.rem(rank + k, count) * rows
        piece = lax.dynamic_slice_in_dim(part, place, rows, 1)
        got = lax.ppermute(piece, "tp", [(i, (i + k) % count) for i in range(count)])
        total = total + got.astype(F32)
    return total


def dot(spec, a, b):
    return jnp.einsum(spec, a, b, preferred_element_type=F32)


def per_device(
    tokens_in,
    out_grad,
    segment_ids,
    expert_ids,
    attn_gain,
    w_query,
    w_key,
    w_value,
    w_output,
    ffn_gain,
    w_router,
    w_gate,
    w_up,
    w_down,
):
    tensor_count = lax.axis_size("tp")
    tensor_rank = lax.axis_index("tp")
    micro, own_rows, width = tokens_in.shape
    group_rows = own_rows * tensor_count
    experts = w_gate.shape[0]
    units = w_gate.shape[2]
    head_width = w_query.shape[1]
    heads = head_width // HD
    query_scale = 1.0 / math.sqrt(HD)
    rows = micro * group_rows
    slots = micro * CAP

    own_small = jnp.concatenate([attn_gain[:, None], ffn_gain[:, None], w_router], axis=1)
    small_rows, small_width = own_small.shape
    shard_rows = w_query.shape[0]
    own_small = jnp.pad(own_small, ((0, shard_rows - small_rows), (0, HD - small_width)))
    attn_set = lax.all_gather(
        jnp.concatenate([w_query, w_key, w_value, w_output.T, own_small], axis=1),
        "fsdp",
        axis=0,
        tiled=True,
    )
    span = 3 * units
    pair_sets = []
    for pair in range(experts // PAIR):
        held = []
        for e in range(pair * PAIR, (pair + 1) * PAIR):
            held += [w_gate[e], w_up[e], w_down[e].T]
        pair_sets.append(lax.all_gather(jnp.concatenate(held, axis=1), "fsdp", axis=0, tiled=True))
    small = attn_set[:, 4 * head_width :].reshape(-1, shard_rows, HD)[:, :small_rows]
    small = tp_gather(small).reshape(width, HD)
    gain_one = small[:, 0].astype(F32)
    gain_two = small[:, 1].astype(F32)
    router = small[:, 2:small_width]

    tokens_full = tp_gather(tokens_in).astype(F32)
    hidden_one = (tokens_full * inverse_rms(tokens_full) * gain_one).astype(BF16)
    hidden_one = hidden_one.reshape(rows, width)
    cosine_table, sine_table = rotary_tables(segment_ids, HD)
    allowed = attend_mask(segment_ids)
    qkv = dot("td,de->te", hidden_one, attn_set[:, : 3 * head_width])
    four = (micro, group_rows, heads, HD)
    query_raw = qkv[:, :head_width].reshape(four)
    key_raw = qkv[:, head_width : 2 * head_width].reshape(four)
    values_low = qkv[:, 2 * head_width :].reshape(four).astype(BF16)
    query_rot = (rotate(query_raw, cosine_table, sine_table) * query_scale).astype(BF16)
    keys_rot = rotate(key_raw, cosine_table, sine_table).astype(BF16)
    scores = dot("mqhd,mkhd->mhqk", query_rot, keys_rot)
    scores = jnp.where(allowed[:, None], scores, MASKED)
    exps = jnp.exp(scores - jnp.max(scores, axis=-1, keepdims=True))
    probs = exps / jnp.sum(exps, axis=-1, keepdims=True)
    probs_low = probs.astype(BF16)
    context = dot("mhqk,mkhd->mqhd", probs_low, values_low).reshape(rows, head_width).astype(BF16)
    attn_part = dot("te,de->td", context, attn_set[:, 3 * head_width : 4 * head_width]).astype(BF16)
    inputs = tokens_in.astype(F32)
    middle = inputs + tp_scatter(attn_part.reshape(micro, group_rows, width))
    normed_two = (middle * inverse_rms(middle) * gain_two).astype(BF16)
    hidden_two = tp_gather(normed_two)
    grad_full = tp_gather(out_grad)

    logits = dot("mtd,de->mte", hidden_two, router)
    named = jnp.any(
        expert_ids[:, :, :, None] == jnp.arange(experts, dtype=jnp.int32), axis=2
    )
    chosen = jnp.where(named, logits, MASKED)
    chosen_exp = jnp.where(named, jnp.exp(chosen - jnp.max(chosen, axis=-1, keepdims=True)), 0.0)
    gates = chosen_exp / jnp.sum(chosen_exp, axis=-1, keepdims=True)
    row_index = jnp.arange(group_rows, dtype=jnp.int32)
    before = (row_index[None, :] < row_index[:, None]).astype(BF16)
    slot_of = dot("ts,mse->met", before, named.astype(BF16)).astype(jnp.int32)
    slot_of = jnp.where(jnp.swapaxes(named, 1, 2), slot_of, -1)
    picks = slot_of[:, :, None, :] == jnp.arange(CAP, dtype=jnp.int32)[None, None, :, None]
    slot_gates = jnp.sum(
        jnp.where(picks, jnp.swapaxes(gates, 1, 2)[:, :, None, :], 0.0), axis=-1, keepdims=True
    )
    picks_low = picks.astype(BF16)

    weighted_outs = []
    gate_grad_slots = []
    routed_grads = []
    pair_grads = []
    pieces = []
    for e in range(experts):
        weights = pair_sets[e // PAIR]
        start = e % PAIR * span
        gate_up = weights[:, start : start + 2 * units]
        down = weights[:, start + 2 * units : start + span]
        pick = picks_low[:, e]
        if e and e % PAIR == 0:
            pick, packed = lax.optimization_barrier((pick, jnp.concatenate(pieces, axis=1)))
            pair_grads.append(lax.psum_scatter(packed, "fsdp", scatter_dimension=0, tiled=True))
            pieces = []
        routed = dot("mst,mtd->msd", pick, hidden_two).astype(BF16).reshape(slots, width)
        grad_slot = dot("mst,mtd->msd", pick, grad_full)
        slot_gate = slot_gates[:, e]
        slot_grad = (slot_gate * grad_slot).astype(BF16).reshape(slots, width)
        pre = dot("sd,df->sf", routed, gate_up)
        gate_pre = pre[:, :units]
        up_pre = pre[:, units:]
        gate_sigmoid = jax.nn.sigmoid(gate_pre)
        silu = gate_pre * gate_sigmoid
        activated = (silu * up_pre).astype(BF16)
        expert_out = dot("sf,df->sd", activated, down).reshape(micro, CAP, width)
        weighted_outs.append((slot_gate * expert_out).astype(BF16))
        gate_grad_slots.append(jnp.sum(expert_out * grad_slot, axis=-1))
        act_grad = dot("sd,df->sf", slot_grad, down)
        pre_grad = jnp.concatenate(
            [
                (act_grad * up_pre * gate_sigmoid * (1.0 + gate_pre * (1.0 - gate_sigmoid))).astype(
                    BF16
                ),
                (act_grad * silu).astype(BF16),
            ],
            axis=1,
        )
        pieces.append(dot("sd,sf->df", routed, pre_grad).astype(BF16))
        pieces.append(dot("sd,sf->df", slot_grad, activated).astype(BF16))
        routed_grads.append(
            dot("sf,df->sd", pre_grad, gate_up).astype(BF16).reshape(micro, CAP, width)
        )
    picks_low, packed = lax.optimization_barrier((picks_low, jnp.concatenate(pieces, axis=1)))
    pair_grads.append(lax.psum_scatter(packed, "fsdp", scatter_dimension=0, tiled=True))
    flat_picks = picks_low.reshape(micro, experts * CAP, group_rows)
    token_grad = dot("mst,msd->mtd", flat_picks, jnp.concatenate(routed_grads, axis=1))
    gate_grad_part = jnp.sum(
        jnp.where(picks, jnp.stack(gate_grad_slots, axis=1)[:, :, :, None], 0.0), axis=2
    )
    gate_grad_part = jnp.pad(jnp.swapaxes(gate_grad_part, 1, 2), ((0, 0), (0, 0), (0, HD - experts)))
    summed = tp_scatter(jnp.concatenate([token_grad, gate_grad_part], axis=-1).astype(BF16))
    moe_part = dot("mst,msd->mtd", flat_picks, jnp.concatenate(weighted_outs, axis=1))
    output = (middle + tp_scatter(moe_part.astype(BF16))).astype(BF16)

    gates_own = lax.dynamic_slice_in_dim(gates, tensor_rank * own_rows, own_rows, 1)
    gate_grad = summed[:, :, width : width + experts]
    logit_grad = gates_own * (
        gate_grad - jnp.sum(gates_own * gate_grad, axis=-1, keepdims=True)
    )
    router_grad = jnp.einsum(
        "mtd,mte->de", normed_two.astype(F32), logit_grad, precision=HIGHEST
    )
    hidden_two_grad = summed[:, :, :width] + jnp.einsum(
        "mte,de->mtd", logit_grad, router.astype(F32), precision=HIGHEST
    )
    middle_norm_grad, gain_two_grad = norm_backward(middle, gain_two, hidden_two_grad)
    middle_grad = middle_norm_grad + out_grad.astype(F32)

    attn_grad = tp_gather(middle_grad.astype(BF16)).reshape(rows, width)
    context_grad = dot("td,de->te", attn_grad, attn_set[:, 3 * head_width : 4 * head_width])
    context_grad = context_grad.astype(BF16).reshape(four)
    prob_grad = dot("mqhd,mkhd->mhqk", context_grad, values_low)
    row_delta = jnp.sum(probs * prob_grad, axis=-1, keepdims=True)
    score_grad = (probs * (prob_grad - row_delta)).astype(BF16)
    query_grad = rotate(
        dot("mhqk,mkhd->mqhd", score_grad, keys_rot) * query_scale, cosine_table, -sine_table
    )
    key_grad = rotate(dot("mhqk,mqhd->mkhd", score_grad, query_rot), cosine_table, -sine_table)
    value_grad = dot("mhqk,mqhd->mkhd", probs_low, context_grad)
    qkv_grad = jnp.concatenate(
        [item.astype(BF16).reshape(rows, head_width) for item in (query_grad, key_grad, value_grad)],
        axis=1,
    )
    hidden_part = dot("te,de->td", qkv_grad, attn_set[:, : 3 * head_width]).astype(BF16)
    hidden_one_grad = tp_scatter(hidden_part.reshape(micro, group_rows, width))
    inner_grad, gain_one_grad = norm_backward(inputs, gain_one, hidden_one_grad)
    input_grad = (middle_grad + inner_grad).astype(BF16)
    small_part = jnp.concatenate(
        [gain_one_grad[:, None], gain_two_grad[:, None], router_grad], axis=1
    )
    attn_packed = jnp.concatenate(
        [
            dot("td,te->de", hidden_one, qkv_grad).astype(BF16),
            dot("td,te->de", attn_grad, context).astype(BF16),
            jnp.pad(small_part, ((0, 0), (0, HD - small_width))).astype(BF16),
        ],
        axis=1,
    )
    attn_packed, pair_grads = lax.optimization_barrier((attn_packed, pair_grads))
    attn_grads = lax.psum_scatter(attn_packed, "fsdp", scatter_dimension=0, tiled=True)
    small_grads = tp_scatter(attn_grads[None, :, 4 * head_width :])[0]
    attn_grads = attn_grads.astype(F32)
    expert_grads = [
        item[:, e * span : (e + 1) * span] for item in pair_grads for e in range(PAIR)
    ]
    return (
        output,
        input_grad,
        small_grads[:, 0],
        attn_grads[:, :head_width],
        attn_grads[:, head_width : 2 * head_width],
        attn_grads[:, 2 * head_width : 3 * head_width],
        attn_grads[:, 3 * head_width : 4 * head_width].T,
        small_grads[:, 1],
        small_grads[:, 2:small_width],
        jnp.stack([item[:, :units] for item in expert_grads]).astype(F32),
        jnp.stack([item[:, units : 2 * units] for item in expert_grads]).astype(F32),
        jnp.stack([item[:, 2 * units :].T for item in expert_grads]).astype(F32),
    )


def solution(mesh):
    return jax.shard_map(
        per_device,
        mesh=mesh,
        in_specs=(
            P(None, ("fsdp", "tp"), None),
            P(None, ("fsdp", "tp"), None),
            P(None, "fsdp"),
            P(None, "fsdp", None),
            P(("fsdp", "tp")),
            P("fsdp", "tp"),
            P("fsdp", "tp"),
            P("fsdp", "tp"),
            P("tp", "fsdp"),
            P(("fsdp", "tp")),
            P(("fsdp", "tp"), None),
            P(None, "fsdp", "tp"),
            P(None, "fsdp", "tp"),
            P(None, "tp", "fsdp"),
        ),
        out_specs=(
            P(None, ("fsdp", "tp"), None),
            P(None, ("fsdp", "tp"), None),
            P(("fsdp", "tp")),
            P("fsdp", "tp"),
            P("fsdp", "tp"),
            P("fsdp", "tp"),
            P("tp", "fsdp"),
            P(("fsdp", "tp")),
            P(("fsdp", "tp"), None),
            P(None, "fsdp", "tp"),
            P(None, "fsdp", "tp"),
            P(None, "tp", "fsdp"),
        ),
        check_vma=False,
    )
```

```python
import math

import jax
import jax.numpy as jnp
from jax import lax
from jax.sharding import PartitionSpec as P


HD = 128
CAP = 200
PAIR = 2
EPSILON = 1e-05
MASKED = -1e30
HIGHEST = lax.Precision.HIGHEST
BF16 = jnp.bfloat16
F32 = jnp.float32


def inverse_rms(values):
    return lax.rsqrt(jnp.mean(values * values, axis=-1, keepdims=True) + EPSILON)


def norm_backward(inputs, gain, grad_out):
    inv_scale = inverse_rms(inputs)
    scaled = grad_out * gain
    input_grad = inv_scale * scaled - inputs * (inv_scale * inv_scale * inv_scale) * jnp.mean(
        scaled * inputs, axis=-1, keepdims=True
    )
    return input_grad


def rotary_tables(segments, head_dim):
    row_index = jnp.arange(segments.shape[1], dtype=jnp.int32)[None, :]
    earlier = jnp.sum((segments[:, None, :] < segments[:, :, None]).astype(jnp.int32), axis=2)
    prompt_rows = jnp.sum((segments == 0).astype(jnp.int32), axis=1, keepdims=True)
    position = row_index - earlier + jnp.where(segments > 0, prompt_rows, 0)
    frequency = 10000.0 ** (-(jnp.arange(head_dim // 2, dtype=F32) * 2.0) / head_dim)
    angles = position.astype(F32)[:, :, None] * frequency[None, None, :]
    return (jnp.cos(angles)[:, :, None, :], jnp.sin(angles)[:, :, None, :])


def rotate(values, cosine_table, sine_table):
    half_dim = values.shape[-1] // 2
    first_half = values[..., :half_dim]
    second_half = values[..., half_dim:]
    return jnp.concatenate(
        [
            first_half * cosine_table - second_half * sine_table,
            second_half * cosine_table + first_half * sine_table,
        ],
        axis=-1,
    )


def attend_mask(segments):
    row_index = jnp.arange(segments.shape[1], dtype=jnp.int32)
    causal = (row_index[None, :] <= row_index[:, None])[None]
    same_doc = (segments[:, None, :] == 0) | (segments[:, None, :] == segments[:, :, None])
    return causal & same_doc


def tp_gather(own, after=None):
    count = lax.axis_size("tp")
    rank = lax.axis_index("tp")
    micro, rows, width = own.shape
    full = jnp.zeros((micro, count * rows, width), own.dtype)
    if after is not None:
        full, _ = lax.optimization_barrier((full, after))
    pieces = [own] + [
        lax.ppermute(own, "tp", [(i, (i + k) % count) for i in range(count)])
        for k in range(1, count)
    ]
    for k, piece in enumerate(pieces):
        place = lax.rem(rank - k + count, count) * rows
        full = lax.dynamic_update_slice_in_dim(full, piece, place, 1)
    return full


def tp_gather_small(own):
    count = lax.axis_size("tp")
    rank = lax.axis_index("tp")
    pieces = [own] + [
        lax.ppermute(own, "tp", [(i, (i + k) % count) for i in range(count)])
        for k in range(1, count)
    ]
    ordered = []
    for place in range(count):
        value = pieces[0]
        for k in range(1, count):
            value = jnp.where(lax.rem(rank - k + count, count) == place, pieces[k], value)
        ordered.append(value)
    return jnp.stack(ordered)


def fsdp_gather(own):
    count = lax.axis_size("fsdp")
    if count != 8:
        full = lax.all_gather(own, "fsdp", axis=0, tiled=True)
        return full, own
    rank = lax.axis_index("fsdp")
    odd = lax.rem(rank, 2) == 1

    def swap(value, bits):
        return lax.ppermute(value, "fsdp", [(i, i ^ bits(i)) for i in range(count)])

    near = swap(own, lambda i: 2)
    far = swap(own, lambda i: 4)
    held = [(0, own), (2, near), (4, far)]
    passed = jnp.where(odd, near, far)
    held.append((6, swap(passed, lambda i: 4 if i % 2 else 2)))
    full = jnp.zeros((count,) + own.shape, own.dtype)
    for bits, value in held:
        full = lax.dynamic_update_index_in_dim(full, value, rank ^ bits, 0)
        other = swap(value, lambda i: 1)
        full = lax.dynamic_update_index_in_dim(full, other, rank ^ (bits | 1), 0)
    return full.reshape(count * own.shape[0], own.shape[1]), passed


def tp_scatter(part):
    count = lax.axis_size("tp")
    rank = lax.axis_index("tp")
    rows = part.shape[1] // count
    total = lax.dynamic_slice_in_dim(part, rank * rows, rows, 1).astype(F32)
    for k in range(1, count):
        place = lax.rem(rank + k, count) * rows
        piece = lax.dynamic_slice_in_dim(part, place, rows, 1)
        got = lax.ppermute(piece, "tp", [(i, (i + k) % count) for i in range(count)])
        total = total + got.astype(F32)
    return total


def dot(spec, a, b):
    return jnp.einsum(spec, a, b, preferred_element_type=F32)


def per_device(
    tokens_in,
    out_grad,
    segment_ids,
    expert_ids,
    attn_gain,
    w_query,
    w_key,
    w_value,
    w_output,
    ffn_gain,
    w_router,
    w_gate,
    w_up,
    w_down,
):
    tensor_count = lax.axis_size("tp")
    tensor_rank = lax.axis_index("tp")
    micro, own_rows, width = tokens_in.shape
    group_rows = own_rows * tensor_count
    experts = w_gate.shape[0]
    units = w_gate.shape[2]
    head_width = w_query.shape[1]
    heads = head_width // HD
    query_scale = 1.0 / math.sqrt(HD)
    rows = micro * group_rows
    slots = micro * CAP

    own_small = jnp.concatenate([attn_gain[:, None], ffn_gain[:, None], w_router], axis=1)
    small_rows, small_width = own_small.shape
    shard_rows = w_query.shape[0]
    own_small = jnp.pad(own_small, ((0, shard_rows - small_rows), (0, HD - small_width)))
    attn_set, passed = fsdp_gather(
        jnp.concatenate([w_query, w_key, w_value, w_output.T, own_small], axis=1)
    )
    span = 3 * units
    pair_sets = []
    for pair in range(experts // PAIR):
        held = []
        for e in range(pair * PAIR, (pair + 1) * PAIR):
            held += [w_gate[e], w_up[e], w_down[e].T]
        if pair:
            held, _ = lax.optimization_barrier((held, joined))
        joined = jnp.concatenate(held, axis=1)
        pair_sets.append(lax.all_gather(joined, "fsdp", axis=0, tiled=True))
    small = attn_set[:, 4 * head_width :].reshape(-1, shard_rows, HD)[:, :small_rows]
    small = tp_gather_small(small.reshape(-1, HD))
    small = small.reshape(tensor_count, -1, small_rows, HD).swapaxes(0, 1).reshape(width, HD)
    gain_one = small[:, 0].astype(F32)
    gain_two = small[:, 1].astype(F32)
    router = small[:, 2:small_width]

    tokens_full = tp_gather(tokens_in, passed).astype(F32)
    hidden_one = (tokens_full * inverse_rms(tokens_full) * gain_one).astype(BF16)
    hidden_one = hidden_one.reshape(rows, width)
    cosine_table, sine_table = rotary_tables(segment_ids, HD)
    allowed = attend_mask(segment_ids)
    qkv = dot("td,de->te", hidden_one, attn_set[:, : 3 * head_width])
    four = (micro, group_rows, heads, HD)
    query_raw = qkv[:, :head_width].reshape(four)
    key_raw = qkv[:, head_width : 2 * head_width].reshape(four)
    values_low = qkv[:, 2 * head_width :].reshape(four).astype(BF16)
    query_rot = (rotate(query_raw, cosine_table, sine_table) * query_scale).astype(BF16)
    keys_rot = rotate(key_raw, cosine_table, sine_table).astype(BF16)
    scores = dot("mqhd,mkhd->mhqk", query_rot, keys_rot)
    scores = jnp.where(allowed[:, None], scores, MASKED)
    exps = jnp.exp(scores - jnp.max(scores, axis=-1, keepdims=True))
    probs = exps / jnp.sum(exps, axis=-1, keepdims=True)
    probs_low = probs.astype(BF16)
    context = dot("mhqk,mkhd->mqhd", probs_low, values_low).reshape(rows, head_width).astype(BF16)
    attn_part = dot("te,de->td", context, attn_set[:, 3 * head_width : 4 * head_width]).astype(BF16)
    inputs = tokens_in.astype(F32)
    middle = inputs + tp_scatter(attn_part.reshape(micro, group_rows, width))
    normed_two = (middle * inverse_rms(middle) * gain_two).astype(BF16)
    hidden_two = tp_gather(normed_two)
    grad_full = tp_gather(out_grad)

    logits = dot("mtd,de->mte", hidden_two, router)
    named = jnp.any(
        expert_ids[:, :, :, None] == jnp.arange(experts, dtype=jnp.int32), axis=2
    )
    chosen = jnp.where(named, logits, MASKED)
    chosen_exp = jnp.where(named, jnp.exp(chosen - jnp.max(chosen, axis=-1, keepdims=True)), 0.0)
    gates = chosen_exp / jnp.sum(chosen_exp, axis=-1, keepdims=True)
    row_index = jnp.arange(group_rows, dtype=jnp.int32)
    before = (row_index[None, :] < row_index[:, None]).astype(BF16)
    slot_of = dot("ts,mse->met", before, named.astype(BF16)).astype(jnp.int32)
    slot_of = jnp.where(jnp.swapaxes(named, 1, 2), slot_of, -1)
    picks = slot_of[:, :, None, :] == jnp.arange(CAP, dtype=jnp.int32)[None, None, :, None]
    slot_gates = jnp.sum(
        jnp.where(picks, jnp.swapaxes(gates, 1, 2)[:, :, None, :], 0.0), axis=-1, keepdims=True
    )
    picks_low = picks.astype(BF16)

    weighted_outs = []
    gate_grad_slots = []
    routed_grads = []
    pair_grads = []
    pieces = []
    for e in range(experts):
        weights = pair_sets[e // PAIR]
        start = e % PAIR * span
        gate_up = weights[:, start : start + 2 * units]
        down = weights[:, start + 2 * units : start + span]
        pick = picks_low[:, e]
        if e and e % PAIR == 0:
            pick, packed, weighted_outs, gate_grad_slots, routed_grads = lax.optimization_barrier(
                (
                    pick,
                    jnp.concatenate(pieces, axis=1),
                    weighted_outs,
                    gate_grad_slots,
                    routed_grads,
                )
            )
            pair_grads.append(lax.psum_scatter(packed, "fsdp", scatter_dimension=0, tiled=True))
            pieces = []
        routed = dot("mst,mtd->msd", pick, hidden_two).astype(BF16).reshape(slots, width)
        grad_slot = dot("mst,mtd->msd", pick, grad_full)
        slot_gate = slot_gates[:, e]
        slot_grad = (slot_gate * grad_slot).astype(BF16).reshape(slots, width)
        pre = dot("sd,df->sf", routed, gate_up)
        gate_pre = pre[:, :units]
        up_pre = pre[:, units:]
        gate_sigmoid = jax.nn.sigmoid(gate_pre)
        silu = gate_pre * gate_sigmoid
        activated = (silu * up_pre).astype(BF16)
        expert_out = dot("sf,df->sd", activated, down).reshape(micro, CAP, width)
        weighted_outs.append((slot_gate * expert_out).astype(BF16))
        gate_grad_slots.append(jnp.sum(expert_out * grad_slot, axis=-1))
        act_grad = dot("sd,df->sf", slot_grad, down)
        pre_grad = jnp.concatenate(
            [
                (act_grad * up_pre * gate_sigmoid * (1.0 + gate_pre * (1.0 - gate_sigmoid))).astype(
                    BF16
                ),
                (act_grad * silu).astype(BF16),
            ],
            axis=1,
        )
        pieces.append(dot("sd,sf->df", routed, pre_grad).astype(BF16))
        pieces.append(dot("sd,sf->df", slot_grad, activated).astype(BF16))
        routed_grads.append(
            dot("sf,df->sd", pre_grad, gate_up).astype(BF16).reshape(micro, CAP, width)
        )
    picks_low, packed = lax.optimization_barrier((picks_low, jnp.concatenate(pieces, axis=1)))
    pair_grads.append(lax.psum_scatter(packed, "fsdp", scatter_dimension=0, tiled=True))
    flat_picks = picks_low.reshape(micro, experts * CAP, group_rows)
    token_grad = dot("mst,msd->mtd", flat_picks, jnp.concatenate(routed_grads, axis=1))
    gate_grad_part = jnp.sum(
        jnp.where(picks, jnp.stack(gate_grad_slots, axis=1)[:, :, :, None], 0.0), axis=2
    )
    gate_grad_part = jnp.pad(jnp.swapaxes(gate_grad_part, 1, 2), ((0, 0), (0, 0), (0, HD - experts)))
    summed = tp_scatter(jnp.concatenate([token_grad, gate_grad_part], axis=-1).astype(BF16))
    moe_part = dot("mst,msd->mtd", flat_picks, jnp.concatenate(weighted_outs, axis=1))

    gates_own = lax.dynamic_slice_in_dim(gates, tensor_rank * own_rows, own_rows, 1)
    gate_grad = summed[:, :, width : width + experts]
    logit_grad = gates_own * (
        gate_grad - jnp.sum(gates_own * gate_grad, axis=-1, keepdims=True)
    )
    router_grad = jnp.einsum(
        "mtd,mte->de", normed_two.astype(F32), logit_grad, precision=HIGHEST
    )
    hidden_two_grad = summed[:, :, :width] + jnp.einsum(
        "mte,de->mtd", logit_grad, router.astype(F32), precision=HIGHEST
    )
    gain_two_grad = jnp.sum(hidden_two_grad * middle * inverse_rms(middle), axis=(0, 1))
    middle_grad = norm_backward(middle, gain_two, hidden_two_grad) + out_grad.astype(F32)

    attn_grad = tp_gather(middle_grad.astype(BF16)).reshape(rows, width)
    moe_low, middle_late, _ = lax.optimization_barrier((moe_part.astype(BF16), middle, attn_grad))
    moe_own = tp_scatter(moe_low)
    output = (middle_late + moe_own).astype(BF16)
    context_grad = dot("td,de->te", attn_grad, attn_set[:, 3 * head_width : 4 * head_width])
    context_grad = context_grad.astype(BF16).reshape(four)
    prob_grad = dot("mqhd,mkhd->mhqk", context_grad, values_low)
    row_delta = jnp.sum(probs * prob_grad, axis=-1, keepdims=True)
    score_grad = (probs * (prob_grad - row_delta)).astype(BF16)
    query_grad = rotate(
        dot("mhqk,mkhd->mqhd", score_grad, keys_rot) * query_scale, cosine_table, -sine_table
    )
    key_grad = rotate(dot("mhqk,mqhd->mkhd", score_grad, query_rot), cosine_table, -sine_table)
    value_grad = dot("mhqk,mqhd->mkhd", probs_low, context_grad)
    qkv_grad = jnp.concatenate(
        [item.astype(BF16).reshape(rows, head_width) for item in (query_grad, key_grad, value_grad)],
        axis=1,
    )
    hidden_part = dot("te,de->td", qkv_grad, attn_set[:, : 3 * head_width])
    hidden_part = hidden_part.reshape(micro, group_rows, width)
    gain_one_grad = jnp.sum(hidden_part * tokens_full * inverse_rms(tokens_full), axis=(0, 1))
    hidden_one_grad = tp_scatter(hidden_part.astype(BF16))
    inner_grad = norm_backward(inputs, gain_one, hidden_one_grad)
    input_grad = (middle_grad + inner_grad).astype(BF16)
    small_part = jnp.concatenate(
        [gain_one_grad[:, None], gain_two_grad[:, None], router_grad], axis=1
    )
    attn_packed = jnp.concatenate(
        [
            dot("td,te->de", hidden_one, qkv_grad).astype(BF16),
            dot("td,te->de", attn_grad, context).astype(BF16),
            jnp.pad(small_part, ((0, 0), (0, HD - small_width))).astype(BF16),
        ],
        axis=1,
    )
    attn_packed, pair_grads, output = lax.optimization_barrier((attn_packed, pair_grads, output))
    attn_grads = lax.psum_scatter(attn_packed, "fsdp", scatter_dimension=0, tiled=True)
    small_grads = tp_scatter(attn_grads[None, :, 4 * head_width :])[0]
    attn_grads = attn_grads.astype(F32)
    expert_grads = [
        item[:, e * span : (e + 1) * span] for item in pair_grads for e in range(PAIR)
    ]
    return (
        output,
        input_grad,
        small_grads[:, 0],
        attn_grads[:, :head_width],
        attn_grads[:, head_width : 2 * head_width],
        attn_grads[:, 2 * head_width : 3 * head_width],
        attn_grads[:, 3 * head_width : 4 * head_width].T,
        small_grads[:, 1],
        small_grads[:, 2:small_width],
        jnp.stack([item[:, :units] for item in expert_grads]).astype(F32),
        jnp.stack([item[:, units : 2 * units] for item in expert_grads]).astype(F32),
        jnp.stack([item[:, 2 * units :].T for item in expert_grads]).astype(F32),
    )


def solution(mesh):
    return jax.shard_map(
        per_device,
        mesh=mesh,
        in_specs=(
            P(None, ("fsdp", "tp"), None),
            P(None, ("fsdp", "tp"), None),
            P(None, "fsdp"),
            P(None, "fsdp", None),
            P(("fsdp", "tp")),
            P("fsdp", "tp"),
            P("fsdp", "tp"),
            P("fsdp", "tp"),
            P("tp", "fsdp"),
            P(("fsdp", "tp")),
            P(("fsdp", "tp"), None),
            P(None, "fsdp", "tp"),
            P(None, "fsdp", "tp"),
            P(None, "tp", "fsdp"),
        ),
        out_specs=(
            P(None, ("fsdp", "tp"), None),
            P(None, ("fsdp", "tp"), None),
            P(("fsdp", "tp")),
            P("fsdp", "tp"),
            P("fsdp", "tp"),
            P("fsdp", "tp"),
            P("tp", "fsdp"),
            P(("fsdp", "tp")),
            P(("fsdp", "tp"), None),
            P(None, "fsdp", "tp"),
            P(None, "fsdp", "tp"),
            P(None, "tp", "fsdp"),
        ),
        check_vma=False,
    )
```

```python
import math

import jax
import jax.numpy as jnp
from jax import lax
from jax.sharding import PartitionSpec as P


HD = 128
CAP = 200
PAIR = 2
EPSILON = 1e-05
MASKED = -1e30
HIGHEST = lax.Precision.HIGHEST
BF16 = jnp.bfloat16
F32 = jnp.float32


def inverse_rms(values):
    return lax.rsqrt(jnp.mean(values * values, axis=-1, keepdims=True) + EPSILON)


def norm_backward(inputs, gain, grad_out):
    inv_scale = inverse_rms(inputs)
    scaled = grad_out * gain
    input_grad = inv_scale * scaled - inputs * (inv_scale * inv_scale * inv_scale) * jnp.mean(
        scaled * inputs, axis=-1, keepdims=True
    )
    return input_grad


def rotary_tables(segments, head_dim):
    row_index = jnp.arange(segments.shape[1], dtype=jnp.int32)[None, :]
    earlier = jnp.sum((segments[:, None, :] < segments[:, :, None]).astype(jnp.int32), axis=2)
    prompt_rows = jnp.sum((segments == 0).astype(jnp.int32), axis=1, keepdims=True)
    position = row_index - earlier + jnp.where(segments > 0, prompt_rows, 0)
    frequency = 10000.0 ** (-(jnp.arange(head_dim // 2, dtype=F32) * 2.0) / head_dim)
    angles = position.astype(F32)[:, :, None] * frequency[None, None, :]
    return (jnp.cos(angles)[:, :, None, :], jnp.sin(angles)[:, :, None, :])


def rotate(values, cosine_table, sine_table):
    half_dim = values.shape[-1] // 2
    first_half = values[..., :half_dim]
    second_half = values[..., half_dim:]
    return jnp.concatenate(
        [
            first_half * cosine_table - second_half * sine_table,
            second_half * cosine_table + first_half * sine_table,
        ],
        axis=-1,
    )


def attend_mask(segments):
    row_index = jnp.arange(segments.shape[1], dtype=jnp.int32)
    causal = (row_index[None, :] <= row_index[:, None])[None]
    same_doc = (segments[:, None, :] == 0) | (segments[:, None, :] == segments[:, :, None])
    return causal & same_doc


def tp_gather(own, after=None):
    count = lax.axis_size("tp")
    rank = lax.axis_index("tp")
    micro, rows, width = own.shape
    full = jnp.zeros((micro, count * rows, width), own.dtype)
    if after is not None:
        full, _ = lax.optimization_barrier((full, after))
    pieces = [own] + [
        lax.ppermute(own, "tp", [(i, (i + k) % count) for i in range(count)])
        for k in range(1, count)
    ]
    for k, piece in enumerate(pieces):
        place = lax.rem(rank - k + count, count) * rows
        full = lax.dynamic_update_slice_in_dim(full, piece, place, 1)
    return full


def tp_gather_small(own):
    count = lax.axis_size("tp")
    rank = lax.axis_index("tp")
    pieces = [own] + [
        lax.ppermute(own, "tp", [(i, (i + k) % count) for i in range(count)])
        for k in range(1, count)
    ]
    ordered = []
    for place in range(count):
        value = pieces[0]
        for k in range(1, count):
            value = jnp.where(lax.rem(rank - k + count, count) == place, pieces[k], value)
        ordered.append(value)
    return jnp.stack(ordered)


def fsdp_gather(own):
    count = lax.axis_size("fsdp")
    if count != 8:
        full = lax.all_gather(own, "fsdp", axis=0, tiled=True)
        return full, own
    rank = lax.axis_index("fsdp")
    odd = lax.rem(rank, 2) == 1

    def swap(value, bits):
        return lax.ppermute(value, "fsdp", [(i, i ^ bits(i)) for i in range(count)])

    near = swap(own, lambda i: 2)
    far = swap(own, lambda i: 4)
    held = [(0, own), (2, near), (4, far)]
    passed = jnp.where(odd, near, far)
    held.append((6, swap(passed, lambda i: 4 if i % 2 else 2)))
    full = jnp.zeros((count,) + own.shape, own.dtype)
    for bits, value in held:
        full = lax.dynamic_update_index_in_dim(full, value, rank ^ bits, 0)
        other = swap(value, lambda i: 1)
        full = lax.dynamic_update_index_in_dim(full, other, rank ^ (bits | 1), 0)
    return full.reshape(count * own.shape[0], own.shape[1]), passed


def tp_scatter(part):
    count = lax.axis_size("tp")
    rank = lax.axis_index("tp")
    rows = part.shape[1] // count
    total = lax.dynamic_slice_in_dim(part, rank * rows, rows, 1).astype(F32)
    for k in range(1, count):
        place = lax.rem(rank + k, count) * rows
        piece = lax.dynamic_slice_in_dim(part, place, rows, 1)
        got = lax.ppermute(piece, "tp", [(i, (i + k) % count) for i in range(count)])
        total = total + got.astype(F32)
    return total


def dot(spec, a, b):
    return jnp.einsum(spec, a, b, preferred_element_type=F32)


def per_device(
    tokens_in,
    out_grad,
    segment_ids,
    expert_ids,
    attn_gain,
    w_query,
    w_key,
    w_value,
    w_output,
    ffn_gain,
    w_router,
    w_gate,
    w_up,
    w_down,
):
    tensor_count = lax.axis_size("tp")
    tensor_rank = lax.axis_index("tp")
    micro, own_rows, width = tokens_in.shape
    group_rows = own_rows * tensor_count
    experts = w_gate.shape[0]
    units = w_gate.shape[2]
    head_width = w_query.shape[1]
    heads = head_width // HD
    query_scale = 1.0 / math.sqrt(HD)
    rows = micro * group_rows
    slots = micro * CAP

    own_small = jnp.concatenate([attn_gain[:, None], ffn_gain[:, None], w_router], axis=1)
    small_rows, small_width = own_small.shape
    shard_rows = w_query.shape[0]
    own_small = jnp.pad(own_small, ((0, shard_rows - small_rows), (0, HD - small_width)))
    attn_set, passed = fsdp_gather(
        jnp.concatenate([w_query, w_key, w_value, w_output.T, own_small], axis=1)
    )
    span = 3 * units
    pair_sets = []
    for pair in range(experts // PAIR):
        held = []
        for e in range(pair * PAIR, (pair + 1) * PAIR):
            held += [w_gate[e], w_up[e], w_down[e].T]
        if pair:
            held, _ = lax.optimization_barrier((held, joined))
        joined = jnp.concatenate(held, axis=1)
        pair_sets.append(lax.all_gather(joined, "fsdp", axis=0, tiled=True))
    small = attn_set[:, 4 * head_width :].reshape(-1, shard_rows, HD)[:, :small_rows]
    small = tp_gather_small(small.reshape(-1, HD))
    small = small.reshape(tensor_count, -1, small_rows, HD).swapaxes(0, 1).reshape(width, HD)
    gain_one = small[:, 0].astype(F32)
    gain_two = small[:, 1].astype(F32)
    router = small[:, 2:small_width]

    tokens_full = tp_gather(tokens_in, passed).astype(F32)
    hidden_one = (tokens_full * inverse_rms(tokens_full) * gain_one).astype(BF16)
    hidden_one = hidden_one.reshape(rows, width)
    cosine_table, sine_table = rotary_tables(segment_ids, HD)
    allowed = attend_mask(segment_ids)
    qkv = dot("td,de->te", hidden_one, attn_set[:, : 3 * head_width])
    four = (micro, group_rows, heads, HD)
    query_raw = qkv[:, :head_width].reshape(four)
    key_raw = qkv[:, head_width : 2 * head_width].reshape(four)
    values_low = qkv[:, 2 * head_width :].reshape(four).astype(BF16)
    query_rot = (rotate(query_raw, cosine_table, sine_table) * query_scale).astype(BF16)
    keys_rot = rotate(key_raw, cosine_table, sine_table).astype(BF16)
    scores = dot("mqhd,mkhd->mhqk", query_rot, keys_rot)
    scores = jnp.where(allowed[:, None], scores, MASKED)
    exps = jnp.exp(scores - jnp.max(scores, axis=-1, keepdims=True))
    probs = exps / jnp.sum(exps, axis=-1, keepdims=True)
    probs_low = probs.astype(BF16)
    context = dot("mhqk,mkhd->mqhd", probs_low, values_low).reshape(rows, head_width).astype(BF16)
    attn_part = dot("te,de->td", context, attn_set[:, 3 * head_width : 4 * head_width]).astype(BF16)
    inputs = tokens_in.astype(F32)
    middle = inputs + tp_scatter(attn_part.reshape(micro, group_rows, width))
    normed_two = (middle * inverse_rms(middle) * gain_two).astype(BF16)
    hidden_two = tp_gather(normed_two)
    grad_full = tp_gather(out_grad)

    logits = dot("mtd,de->mte", hidden_two, router)
    named = jnp.any(
        expert_ids[:, :, :, None] == jnp.arange(experts, dtype=jnp.int32), axis=2
    )
    chosen = jnp.where(named, logits, MASKED)
    chosen_exp = jnp.where(named, jnp.exp(chosen - jnp.max(chosen, axis=-1, keepdims=True)), 0.0)
    gates = chosen_exp / jnp.sum(chosen_exp, axis=-1, keepdims=True)
    row_index = jnp.arange(group_rows, dtype=jnp.int32)
    before = (row_index[None, :] < row_index[:, None]).astype(BF16)
    slot_of = dot("ts,mse->met", before, named.astype(BF16)).astype(jnp.int32)
    slot_of = jnp.where(jnp.swapaxes(named, 1, 2), slot_of, -1)
    picks = slot_of[:, :, None, :] == jnp.arange(CAP, dtype=jnp.int32)[None, None, :, None]
    slot_gates = jnp.sum(
        jnp.where(picks, jnp.swapaxes(gates, 1, 2)[:, :, None, :], 0.0), axis=-1, keepdims=True
    )
    picks_low = picks.astype(BF16)

    weighted_outs = []
    gate_grad_slots = []
    routed_grads = []
    pair_grads = []
    pieces = []
    for e in range(experts):
        weights = pair_sets[e // PAIR]
        start = e % PAIR * span
        gate_up = weights[:, start : start + 2 * units]
        down = weights[:, start + 2 * units : start + span]
        pick = picks_low[:, e]
        if e and e % PAIR == 0:
            pick, packed = lax.optimization_barrier((pick, jnp.concatenate(pieces, axis=1)))
            pair_grads.append(lax.psum_scatter(packed, "fsdp", scatter_dimension=0, tiled=True))
            pieces = []
        routed = dot("mst,mtd->msd", pick, hidden_two).astype(BF16).reshape(slots, width)
        grad_slot = dot("mst,mtd->msd", pick, grad_full)
        slot_gate = slot_gates[:, e]
        slot_grad = (slot_gate * grad_slot).astype(BF16).reshape(slots, width)
        pre = dot("sd,df->sf", routed, gate_up)
        gate_pre = pre[:, :units]
        up_pre = pre[:, units:]
        gate_sigmoid = jax.nn.sigmoid(gate_pre)
        silu = gate_pre * gate_sigmoid
        activated = (silu * up_pre).astype(BF16)
        expert_out = dot("sf,df->sd", activated, down).reshape(micro, CAP, width)
        weighted_outs.append((slot_gate * expert_out).astype(BF16))
        gate_grad_slots.append(jnp.sum(expert_out * grad_slot, axis=-1))
        act_grad = dot("sd,df->sf", slot_grad, down)
        pre_grad = jnp.concatenate(
            [
                (act_grad * up_pre * gate_sigmoid * (1.0 + gate_pre * (1.0 - gate_sigmoid))).astype(
                    BF16
                ),
                (act_grad * silu).astype(BF16),
            ],
            axis=1,
        )
        pieces.append(dot("sd,sf->df", routed, pre_grad).astype(BF16))
        pieces.append(dot("sd,sf->df", slot_grad, activated).astype(BF16))
        routed_grads.append(
            dot("sf,df->sd", pre_grad, gate_up).astype(BF16).reshape(micro, CAP, width)
        )
    picks_low, packed = lax.optimization_barrier((picks_low, jnp.concatenate(pieces, axis=1)))
    pair_grads.append(lax.psum_scatter(packed, "fsdp", scatter_dimension=0, tiled=True))
    flat_picks = picks_low.reshape(micro, experts * CAP, group_rows)
    token_grad = dot("mst,msd->mtd", flat_picks, jnp.concatenate(routed_grads, axis=1))
    gate_grad_part = jnp.sum(
        jnp.where(picks, jnp.stack(gate_grad_slots, axis=1)[:, :, :, None], 0.0), axis=2
    )
    gate_grad_part = jnp.pad(jnp.swapaxes(gate_grad_part, 1, 2), ((0, 0), (0, 0), (0, HD - experts)))
    summed = tp_scatter(jnp.concatenate([token_grad, gate_grad_part], axis=-1).astype(BF16))
    moe_part = dot("mst,msd->mtd", flat_picks, jnp.concatenate(weighted_outs, axis=1))

    gates_own = lax.dynamic_slice_in_dim(gates, tensor_rank * own_rows, own_rows, 1)
    gate_grad = summed[:, :, width : width + experts]
    logit_grad = gates_own * (
        gate_grad - jnp.sum(gates_own * gate_grad, axis=-1, keepdims=True)
    )
    router_grad = jnp.einsum(
        "mtd,mte->de", normed_two.astype(F32), logit_grad, precision=HIGHEST
    )
    hidden_two_grad = summed[:, :, :width] + jnp.einsum(
        "mte,de->mtd", logit_grad, router.astype(F32), precision=HIGHEST
    )
    gain_two_grad = jnp.sum(hidden_two_grad * middle * inverse_rms(middle), axis=(0, 1))
    middle_grad = norm_backward(middle, gain_two, hidden_two_grad) + out_grad.astype(F32)

    attn_grad = tp_gather(middle_grad.astype(BF16)).reshape(rows, width)
    moe_low, middle_late, _ = lax.optimization_barrier((moe_part.astype(BF16), middle, attn_grad))
    moe_own = tp_scatter(moe_low)
    output = (middle_late + moe_own).astype(BF16)
    context_grad = dot("td,de->te", attn_grad, attn_set[:, 3 * head_width : 4 * head_width])
    context_grad = context_grad.astype(BF16).reshape(four)
    prob_grad = dot("mqhd,mkhd->mhqk", context_grad, values_low)
    row_delta = jnp.sum(probs * prob_grad, axis=-1, keepdims=True)
    score_grad = (probs * (prob_grad - row_delta)).astype(BF16)
    query_grad = rotate(
        dot("mhqk,mkhd->mqhd", score_grad, keys_rot) * query_scale, cosine_table, -sine_table
    )
    key_grad = rotate(dot("mhqk,mqhd->mkhd", score_grad, query_rot), cosine_table, -sine_table)
    value_grad = dot("mhqk,mqhd->mkhd", probs_low, context_grad)
    qkv_grad = jnp.concatenate(
        [item.astype(BF16).reshape(rows, head_width) for item in (query_grad, key_grad, value_grad)],
        axis=1,
    )
    hidden_part = dot("te,de->td", qkv_grad, attn_set[:, : 3 * head_width])
    hidden_part = hidden_part.reshape(micro, group_rows, width)
    gain_one_grad = jnp.sum(hidden_part * tokens_full * inverse_rms(tokens_full), axis=(0, 1))
    hidden_one_grad = tp_scatter(hidden_part.astype(BF16))
    inner_grad = norm_backward(inputs, gain_one, hidden_one_grad)
    input_grad = (middle_grad + inner_grad).astype(BF16)
    small_part = jnp.concatenate(
        [gain_one_grad[:, None], gain_two_grad[:, None], router_grad], axis=1
    )
    attn_packed = jnp.concatenate(
        [
            dot("td,te->de", hidden_one, qkv_grad).astype(BF16),
            dot("td,te->de", attn_grad, context).astype(BF16),
            jnp.pad(small_part, ((0, 0), (0, HD - small_width))).astype(BF16),
        ],
        axis=1,
    )
    attn_packed, pair_grads, output = lax.optimization_barrier((attn_packed, pair_grads, output))
    attn_grads = lax.psum_scatter(attn_packed, "fsdp", scatter_dimension=0, tiled=True)
    expert_grads = [
        item[:, e * span : (e + 1) * span] for item in pair_grads for e in range(PAIR)
    ]
    expert_grads = (
        jnp.stack([item[:, :units] for item in expert_grads]).astype(F32),
        jnp.stack([item[:, units : 2 * units] for item in expert_grads]).astype(F32),
        jnp.stack([item[:, 2 * units :].T for item in expert_grads]).astype(F32),
    )
    small_grads, expert_grads = lax.optimization_barrier(
        (attn_grads[None, :, 4 * head_width :], expert_grads)
    )
    small_grads = tp_scatter(small_grads)[0]
    attn_grads = attn_grads.astype(F32)
    return (
        output,
        input_grad,
        small_grads[:, 0],
        attn_grads[:, :head_width],
        attn_grads[:, head_width : 2 * head_width],
        attn_grads[:, 2 * head_width : 3 * head_width],
        attn_grads[:, 3 * head_width : 4 * head_width].T,
        small_grads[:, 1],
        small_grads[:, 2:small_width],
        *expert_grads,
    )


def solution(mesh):
    return jax.shard_map(
        per_device,
        mesh=mesh,
        in_specs=(
            P(None, ("fsdp", "tp"), None),
            P(None, ("fsdp", "tp"), None),
            P(None, "fsdp"),
            P(None, "fsdp", None),
            P(("fsdp", "tp")),
            P("fsdp", "tp"),
            P("fsdp", "tp"),
            P("fsdp", "tp"),
            P("tp", "fsdp"),
            P(("fsdp", "tp")),
            P(("fsdp", "tp"), None),
            P(None, "fsdp", "tp"),
            P(None, "fsdp", "tp"),
            P(None, "tp", "fsdp"),
        ),
        out_specs=(
            P(None, ("fsdp", "tp"), None),
            P(None, ("fsdp", "tp"), None),
            P(("fsdp", "tp")),
            P("fsdp", "tp"),
            P("fsdp", "tp"),
            P("fsdp", "tp"),
            P("tp", "fsdp"),
            P(("fsdp", "tp")),
            P(("fsdp", "tp"), None),
            P(None, "fsdp", "tp"),
            P(None, "fsdp", "tp"),
            P(None, "tp", "fsdp"),
        ),
        check_vma=False,
    )
```

```python
import math

import jax
import jax.numpy as jnp
from jax import lax
from jax.sharding import PartitionSpec as P


HD = 128
CAP = 200
PAIR = 2
EPSILON = 1e-05
MASKED = -1e30
HIGHEST = lax.Precision.HIGHEST
BF16 = jnp.bfloat16
F32 = jnp.float32


def inverse_rms(values):
    return lax.rsqrt(jnp.mean(values * values, axis=-1, keepdims=True) + EPSILON)


def norm_backward(inputs, gain, grad_out):
    inv_scale = inverse_rms(inputs)
    scaled = grad_out * gain
    input_grad = inv_scale * scaled - inputs * (inv_scale * inv_scale * inv_scale) * jnp.mean(
        scaled * inputs, axis=-1, keepdims=True
    )
    return input_grad


def rotary_tables(segments, head_dim):
    row_index = jnp.arange(segments.shape[1], dtype=jnp.int32)[None, :]
    earlier = jnp.sum((segments[:, None, :] < segments[:, :, None]).astype(jnp.int32), axis=2)
    prompt_rows = jnp.sum((segments == 0).astype(jnp.int32), axis=1, keepdims=True)
    position = row_index - earlier + jnp.where(segments > 0, prompt_rows, 0)
    frequency = 10000.0 ** (-(jnp.arange(head_dim // 2, dtype=F32) * 2.0) / head_dim)
    angles = position.astype(F32)[:, :, None] * frequency[None, None, :]
    return (jnp.cos(angles)[:, :, None, :], jnp.sin(angles)[:, :, None, :])


def rotate(values, cosine_table, sine_table):
    half_dim = values.shape[-1] // 2
    first_half = values[..., :half_dim]
    second_half = values[..., half_dim:]
    return jnp.concatenate(
        [
            first_half * cosine_table - second_half * sine_table,
            second_half * cosine_table + first_half * sine_table,
        ],
        axis=-1,
    )


def attend_mask(segments):
    row_index = jnp.arange(segments.shape[1], dtype=jnp.int32)
    causal = (row_index[None, :] <= row_index[:, None])[None]
    same_doc = (segments[:, None, :] == 0) | (segments[:, None, :] == segments[:, :, None])
    return causal & same_doc


def tp_gather(own, after=None):
    count = lax.axis_size("tp")
    rank = lax.axis_index("tp")
    micro, rows, width = own.shape
    full = jnp.zeros((micro, count * rows, width), own.dtype)
    if after is not None:
        full, _ = lax.optimization_barrier((full, after))
    pieces = [own] + [
        lax.ppermute(own, "tp", [(i, (i + k) % count) for i in range(count)])
        for k in range(1, count)
    ]
    for k, piece in enumerate(pieces):
        place = lax.rem(rank - k + count, count) * rows
        full = lax.dynamic_update_slice_in_dim(full, piece, place, 1)
    return full


def tp_gather_small(own):
    count = lax.axis_size("tp")
    rank = lax.axis_index("tp")
    pieces = [own] + [
        lax.ppermute(own, "tp", [(i, (i + k) % count) for i in range(count)])
        for k in range(1, count)
    ]
    ordered = []
    for place in range(count):
        value = pieces[0]
        for k in range(1, count):
            value = jnp.where(lax.rem(rank - k + count, count) == place, pieces[k], value)
        ordered.append(value)
    return jnp.stack(ordered)


def fsdp_gather(own):
    count = lax.axis_size("fsdp")
    if count != 8:
        full = lax.all_gather(own, "fsdp", axis=0, tiled=True)
        return full, own
    rank = lax.axis_index("fsdp")
    odd = lax.rem(rank, 2) == 1

    def swap(value, bits):
        return lax.ppermute(value, "fsdp", [(i, i ^ bits(i)) for i in range(count)])

    near = swap(own, lambda i: 2)
    far = swap(own, lambda i: 4)
    held = [(0, own), (2, near), (4, far)]
    passed = jnp.where(odd, near, far)
    held.append((6, swap(passed, lambda i: 4 if i % 2 else 2)))
    full = jnp.zeros((count,) + own.shape, own.dtype)
    for bits, value in held:
        full = lax.dynamic_update_index_in_dim(full, value, rank ^ bits, 0)
        other = swap(value, lambda i: 1)
        full = lax.dynamic_update_index_in_dim(full, other, rank ^ (bits | 1), 0)
    return full.reshape(count * own.shape[0], own.shape[1]), passed


def fsdp_scatter(part):
    count = lax.axis_size("fsdp")
    if count != 8:
        return lax.psum_scatter(part, "fsdp", scatter_dimension=0, tiled=True)
    rank = lax.axis_index("fsdp")
    core = lax.rem(rank, 2)
    across = lax.rem(rank // 2, 2)
    along = rank // 4
    even = core == 0

    def swap(value, bits):
        return lax.ppermute(value, "fsdp", [(i, i ^ bits(i)) for i in range(count)])

    def add(a, b):
        return (a.astype(F32) + b.astype(F32)).astype(BF16)

    rows = part.shape[0] // count
    halves = part.reshape(4, 2, rows, part.shape[1])
    sums = add(
        lax.dynamic_index_in_dim(halves, core, 1, keepdims=False),
        swap(lax.dynamic_index_in_dim(halves, 1 - core, 1, keepdims=False), lambda i: 1),
    )
    chosen = jnp.where(even, along, across)
    joined = []
    for kept in (1 - chosen, chosen):
        own = jnp.where(even, kept * 2 + across, along * 2 + kept)
        sent = jnp.where(even, kept * 2 + 1 - across, (1 - along) * 2 + kept)
        joined.append(
            add(
                lax.dynamic_index_in_dim(sums, own, 0, keepdims=False),
                swap(
                    lax.dynamic_index_in_dim(sums, sent, 0, keepdims=False),
                    lambda i: 4 if i % 2 else 2,
                ),
            )
        )
    return add(joined[1], swap(joined[0], lambda i: 2 if i % 2 else 4))


def tp_scatter(part):
    count = lax.axis_size("tp")
    rank = lax.axis_index("tp")
    rows = part.shape[1] // count
    total = lax.dynamic_slice_in_dim(part, rank * rows, rows, 1).astype(F32)
    for k in range(1, count):
        place = lax.rem(rank + k, count) * rows
        piece = lax.dynamic_slice_in_dim(part, place, rows, 1)
        got = lax.ppermute(piece, "tp", [(i, (i + k) % count) for i in range(count)])
        total = total + got.astype(F32)
    return total


def dot(spec, a, b):
    return jnp.einsum(spec, a, b, preferred_element_type=F32)


def per_device(
    tokens_in,
    out_grad,
    segment_ids,
    expert_ids,
    attn_gain,
    w_query,
    w_key,
    w_value,
    w_output,
    ffn_gain,
    w_router,
    w_gate,
    w_up,
    w_down,
):
    tensor_count = lax.axis_size("tp")
    tensor_rank = lax.axis_index("tp")
    micro, own_rows, width = tokens_in.shape
    group_rows = own_rows * tensor_count
    experts = w_gate.shape[0]
    units = w_gate.shape[2]
    head_width = w_query.shape[1]
    heads = head_width // HD
    query_scale = 1.0 / math.sqrt(HD)
    rows = micro * group_rows
    slots = micro * CAP

    own_small = jnp.concatenate([attn_gain[:, None], ffn_gain[:, None], w_router], axis=1)
    small_rows, small_width = own_small.shape
    shard_rows = w_query.shape[0]
    own_small = jnp.pad(own_small, ((0, shard_rows - small_rows), (0, HD - small_width)))
    attn_set, passed = fsdp_gather(
        jnp.concatenate([w_query, w_key, w_value, w_output.T, own_small], axis=1)
    )
    span = 3 * units
    pair_sets = []
    for pair in range(experts // PAIR):
        held = []
        for e in range(pair * PAIR, (pair + 1) * PAIR):
            held += [w_gate[e], w_up[e], w_down[e].T]
        if pair:
            held, _ = lax.optimization_barrier((held, joined))
        joined = jnp.concatenate(held, axis=1)
        pair_sets.append(lax.all_gather(joined, "fsdp", axis=0, tiled=True))
    small = attn_set[:, 4 * head_width :].reshape(-1, shard_rows, HD)[:, :small_rows]
    small = tp_gather_small(small.reshape(-1, HD))
    small = small.reshape(tensor_count, -1, small_rows, HD).swapaxes(0, 1).reshape(width, HD)
    gain_one = small[:, 0].astype(F32)
    gain_two = small[:, 1].astype(F32)
    router = small[:, 2:small_width]

    tokens_full = tp_gather(tokens_in, passed).astype(F32)
    hidden_one = (tokens_full * inverse_rms(tokens_full) * gain_one).astype(BF16)
    hidden_one = hidden_one.reshape(rows, width)
    cosine_table, sine_table = rotary_tables(segment_ids, HD)
    allowed = attend_mask(segment_ids)
    qkv = dot("td,de->te", hidden_one, attn_set[:, : 3 * head_width])
    four = (micro, group_rows, heads, HD)
    query_raw = qkv[:, :head_width].reshape(four)
    key_raw = qkv[:, head_width : 2 * head_width].reshape(four)
    values_low = qkv[:, 2 * head_width :].reshape(four).astype(BF16)
    query_rot = (rotate(query_raw, cosine_table, sine_table) * query_scale).astype(BF16)
    keys_rot = rotate(key_raw, cosine_table, sine_table).astype(BF16)
    scores = dot("mqhd,mkhd->mhqk", query_rot, keys_rot)
    scores = jnp.where(allowed[:, None], scores, MASKED)
    exps = jnp.exp(scores - jnp.max(scores, axis=-1, keepdims=True))
    probs = exps / jnp.sum(exps, axis=-1, keepdims=True)
    probs_low = probs.astype(BF16)
    context = dot("mhqk,mkhd->mqhd", probs_low, values_low).reshape(rows, head_width).astype(BF16)
    attn_part = dot("te,de->td", context, attn_set[:, 3 * head_width : 4 * head_width]).astype(BF16)
    inputs = tokens_in.astype(F32)
    middle = inputs + tp_scatter(attn_part.reshape(micro, group_rows, width))
    normed_two = (middle * inverse_rms(middle) * gain_two).astype(BF16)
    hidden_two = tp_gather(normed_two)
    grad_full = tp_gather(out_grad)

    logits = dot("mtd,de->mte", hidden_two, router)
    named = jnp.any(
        expert_ids[:, :, :, None] == jnp.arange(experts, dtype=jnp.int32), axis=2
    )
    chosen = jnp.where(named, logits, MASKED)
    chosen_exp = jnp.where(named, jnp.exp(chosen - jnp.max(chosen, axis=-1, keepdims=True)), 0.0)
    gates = chosen_exp / jnp.sum(chosen_exp, axis=-1, keepdims=True)
    row_index = jnp.arange(group_rows, dtype=jnp.int32)
    before = (row_index[None, :] < row_index[:, None]).astype(BF16)
    slot_of = dot("ts,mse->met", before, named.astype(BF16)).astype(jnp.int32)
    slot_of = jnp.where(jnp.swapaxes(named, 1, 2), slot_of, -1)
    picks = slot_of[:, :, None, :] == jnp.arange(CAP, dtype=jnp.int32)[None, None, :, None]
    slot_gates = jnp.sum(
        jnp.where(picks, jnp.swapaxes(gates, 1, 2)[:, :, None, :], 0.0), axis=-1, keepdims=True
    )
    picks_low = picks.astype(BF16)

    weighted_outs = []
    gate_grad_slots = []
    routed_grads = []
    pair_grads = []
    pieces = []
    for e in range(experts):
        weights = pair_sets[e // PAIR]
        start = e % PAIR * span
        gate_up = weights[:, start : start + 2 * units]
        down = weights[:, start + 2 * units : start + span]
        pick = picks_low[:, e]
        if e and e % PAIR == 0:
            pick, packed = lax.optimization_barrier((pick, jnp.concatenate(pieces, axis=1)))
            pair_grads.append(lax.psum_scatter(packed, "fsdp", scatter_dimension=0, tiled=True))
            pieces = []
        routed = dot("mst,mtd->msd", pick, hidden_two).astype(BF16).reshape(slots, width)
        grad_slot = dot("mst,mtd->msd", pick, grad_full)
        slot_gate = slot_gates[:, e]
        slot_grad = (slot_gate * grad_slot).astype(BF16).reshape(slots, width)
        pre = dot("sd,df->sf", routed, gate_up)
        gate_pre = pre[:, :units]
        up_pre = pre[:, units:]
        gate_sigmoid = jax.nn.sigmoid(gate_pre)
        silu = gate_pre * gate_sigmoid
        activated = (silu * up_pre).astype(BF16)
        expert_out = dot("sf,df->sd", activated, down).reshape(micro, CAP, width)
        weighted_outs.append((slot_gate * expert_out).astype(BF16))
        gate_grad_slots.append(jnp.sum(expert_out * grad_slot, axis=-1))
        act_grad = dot("sd,df->sf", slot_grad, down)
        pre_grad = jnp.concatenate(
            [
                (act_grad * up_pre * gate_sigmoid * (1.0 + gate_pre * (1.0 - gate_sigmoid))).astype(
                    BF16
                ),
                (act_grad * silu).astype(BF16),
            ],
            axis=1,
        )
        pieces.append(dot("sd,sf->df", routed, pre_grad).astype(BF16))
        pieces.append(dot("sd,sf->df", slot_grad, activated).astype(BF16))
        routed_grads.append(
            dot("sf,df->sd", pre_grad, gate_up).astype(BF16).reshape(micro, CAP, width)
        )
    picks_low, packed = lax.optimization_barrier((picks_low, jnp.concatenate(pieces, axis=1)))
    pair_grads.append(lax.psum_scatter(packed, "fsdp", scatter_dimension=0, tiled=True))
    flat_picks = picks_low.reshape(micro, experts * CAP, group_rows)
    token_grad = dot("mst,msd->mtd", flat_picks, jnp.concatenate(routed_grads, axis=1))
    gate_grad_part = jnp.sum(
        jnp.where(picks, jnp.stack(gate_grad_slots, axis=1)[:, :, :, None], 0.0), axis=2
    )
    gate_grad_part = jnp.pad(jnp.swapaxes(gate_grad_part, 1, 2), ((0, 0), (0, 0), (0, HD - experts)))
    summed = tp_scatter(jnp.concatenate([token_grad, gate_grad_part], axis=-1).astype(BF16))
    moe_part = dot("mst,msd->mtd", flat_picks, jnp.concatenate(weighted_outs, axis=1))

    gates_own = lax.dynamic_slice_in_dim(gates, tensor_rank * own_rows, own_rows, 1)
    gate_grad = summed[:, :, width : width + experts]
    logit_grad = gates_own * (
        gate_grad - jnp.sum(gates_own * gate_grad, axis=-1, keepdims=True)
    )
    router_grad = jnp.einsum(
        "mtd,mte->de", normed_two.astype(F32), logit_grad, precision=HIGHEST
    )
    hidden_two_grad = summed[:, :, :width] + jnp.einsum(
        "mte,de->mtd", logit_grad, router.astype(F32), precision=HIGHEST
    )
    gain_two_grad = jnp.sum(hidden_two_grad * middle * inverse_rms(middle), axis=(0, 1))
    middle_grad = norm_backward(middle, gain_two, hidden_two_grad) + out_grad.astype(F32)

    attn_grad = tp_gather(middle_grad.astype(BF16)).reshape(rows, width)
    moe_low, middle_late, _ = lax.optimization_barrier((moe_part.astype(BF16), middle, attn_grad))
    moe_own = tp_scatter(moe_low)
    output = (middle_late + moe_own).astype(BF16)
    context_grad = dot("td,de->te", attn_grad, attn_set[:, 3 * head_width : 4 * head_width])
    context_grad = context_grad.astype(BF16).reshape(four)
    prob_grad = dot("mqhd,mkhd->mhqk", context_grad, values_low)
    row_delta = jnp.sum(probs * prob_grad, axis=-1, keepdims=True)
    score_grad = (probs * (prob_grad - row_delta)).astype(BF16)
    query_grad = rotate(
        dot("mhqk,mkhd->mqhd", score_grad, keys_rot) * query_scale, cosine_table, -sine_table
    )
    key_grad = rotate(dot("mhqk,mqhd->mkhd", score_grad, query_rot), cosine_table, -sine_table)
    value_grad = dot("mhqk,mqhd->mkhd", probs_low, context_grad)
    qkv_grad = jnp.concatenate(
        [item.astype(BF16).reshape(rows, head_width) for item in (query_grad, key_grad, value_grad)],
        axis=1,
    )
    hidden_part = dot("te,de->td", qkv_grad, attn_set[:, : 3 * head_width])
    hidden_part = hidden_part.reshape(micro, group_rows, width)
    gain_one_grad = jnp.sum(hidden_part * tokens_full * inverse_rms(tokens_full), axis=(0, 1))
    hidden_one_grad = tp_scatter(hidden_part.astype(BF16))
    inner_grad = norm_backward(inputs, gain_one, hidden_one_grad)
    input_grad = (middle_grad + inner_grad).astype(BF16)
    small_part = jnp.concatenate(
        [gain_one_grad[:, None], gain_two_grad[:, None], router_grad], axis=1
    )
    attn_packed = jnp.concatenate(
        [
            dot("td,te->de", hidden_one, qkv_grad).astype(BF16),
            dot("td,te->de", attn_grad, context).astype(BF16),
            jnp.pad(small_part, ((0, 0), (0, HD - small_width))).astype(BF16),
        ],
        axis=1,
    )
    attn_grads = fsdp_scatter(attn_packed)
    small_grads, pair_grads, output, input_grad = lax.optimization_barrier(
        (attn_grads[None, :, 4 * head_width :], pair_grads, output, input_grad)
    )
    small_grads = tp_scatter(small_grads)[0]
    expert_grads = [
        item[:, e * span : (e + 1) * span] for item in pair_grads for e in range(PAIR)
    ]
    expert_grads = (
        jnp.stack([item[:, :units] for item in expert_grads]).astype(F32),
        jnp.stack([item[:, units : 2 * units] for item in expert_grads]).astype(F32),
        jnp.stack([item[:, 2 * units :].T for item in expert_grads]).astype(F32),
    )
    attn_grads = attn_grads.astype(F32)
    return (
        output,
        input_grad,
        small_grads[:, 0],
        attn_grads[:, :head_width],
        attn_grads[:, head_width : 2 * head_width],
        attn_grads[:, 2 * head_width : 3 * head_width],
        attn_grads[:, 3 * head_width : 4 * head_width].T,
        small_grads[:, 1],
        small_grads[:, 2:small_width],
        *expert_grads,
    )


def solution(mesh):
    return jax.shard_map(
        per_device,
        mesh=mesh,
        in_specs=(
            P(None, ("fsdp", "tp"), None),
            P(None, ("fsdp", "tp"), None),
            P(None, "fsdp"),
            P(None, "fsdp", None),
            P(("fsdp", "tp")),
            P("fsdp", "tp"),
            P("fsdp", "tp"),
            P("fsdp", "tp"),
            P("tp", "fsdp"),
            P(("fsdp", "tp")),
            P(("fsdp", "tp"), None),
            P(None, "fsdp", "tp"),
            P(None, "fsdp", "tp"),
            P(None, "tp", "fsdp"),
        ),
        out_specs=(
            P(None, ("fsdp", "tp"), None),
            P(None, ("fsdp", "tp"), None),
            P(("fsdp", "tp")),
            P("fsdp", "tp"),
            P("fsdp", "tp"),
            P("fsdp", "tp"),
            P("tp", "fsdp"),
            P(("fsdp", "tp")),
            P(("fsdp", "tp"), None),
            P(None, "fsdp", "tp"),
            P(None, "fsdp", "tp"),
            P(None, "tp", "fsdp"),
        ),
        check_vma=False,
    )
```
